512 devices in a mesh: tok: 64 (over y, z_lo, x), feat: 8 (over z_hi, core).
Axes of the slice: x: 4, y: 8, z: 8 (z_hi: 4, z_lo: 2; z = z_hi * 2 + z_lo), core: 2. Of those that a mesh axis runs over, the one named last changes fastest.
Arguments:
- hidden_states: bfloat16 [110592, 8192], P('tok', 'feat'), may hold values from -60 to 60
- current_block: float32 [8192, 64], P('feat'), may hold values from -0.0625 to 0.0625
- directions: float32 [8192, 64], P('feat'), may hold values from -0.0625 to 0.0625
Outputs:
- block_image: float32 [8192, 192], P('feat')
- gram_image: float32 [192, 192], replicated
- gram_search: float32 [192, 192], replicated
The draws below stay inside these ranges and needn't reach their ends.
All inputs are finite; a program needn't handle non-finite values.
Results may differ from the reference program's by a relative error of at most 0.005.
Values may be sent and summed in bfloat16 or wider, within the bound.
No kernel may reach another device: no remote copies, remote signals or barrier semaphores. Data moves between devices by JAX's collectives and lax.ppermute only.
A program may use at most 64 MiB of HBM per device.

```python
import math
import jax
import jax.numpy as jnp
from jax import lax

D = 8192
KX = 64
LAG = 256
TOKENS = 110592


def draw_hidden_states(key, part):
    key_base = jax.random.fold_in(key, 11)
    key_rows = jax.random.fold_in(key, 12)
    key_cols = jax.random.fold_in(key, 13)
    position = jnp.arange(TOKENS, dtype=jnp.float32) / TOKENS
    feature = jnp.arange(D, dtype=jnp.float32) / D
    row_scale = jnp.exp(jax.random.uniform(key_rows, (TOKENS, 1), jnp.float32, -1.15, 1.15)) * jnp.sqrt(1.0 + 2.0 * position)[:, None]
    col_scale = jnp.exp(jax.random.uniform(key_cols, (1, D), jnp.float32, -0.69, 0.69)) * jnp.sqrt(1.0 + 2.0 * feature)[None, :]
    base = jnp.clip(jax.random.normal(key_base, (TOKENS, D), jnp.float32), -6.0, 6.0)
    values = jnp.clip(0.5 * base * row_scale * col_scale, -60.0, 60.0)
    return values.astype(jnp.bfloat16)


def block_scale(stream_key, extent, pieces, low, largest):
    factor_of, own = 1.0, jax.random.fold_in(stream_key, 6)
    for axis_at, blocks in pieces:
        steps = jnp.exp(jax.random.uniform(jax.random.fold_in(own, axis_at), (blocks,), jnp.float32, low / len(pieces), largest / len(pieces)))
        factor_of = factor_of * jnp.repeat(steps, extent[axis_at] // blocks).reshape([-1 if axis == axis_at else 1 for axis in range(len(extent))])
    return factor_of


def scatter_about(rng, dims, width, most, cuts=(), held_as=jnp.bfloat16):
    drawn = jax.random.normal(rng, dims, jnp.float32) * width
    if len(cuts) > 0:
        drawn = block_scale(rng, dims, cuts, -0.22, 0.18) * drawn
    return jnp.clip(drawn, min=-most, max=most).astype(held_as)


def setup_inputs(seed: int = 0) -> dict:
    seeds = jax.random.split(jax.random.key(seed), 4)
    return {
        "hidden_states": draw_hidden_states(jax.random.fold_in(seeds[3], 71), 0),
        "current_block": scatter_about(seeds[1], (D, KX), D ** -0.5, 0.0625, ((0, 8),), jnp.float32),
        "directions": scatter_about(seeds[2], (D, KX), D ** -0.5, 0.0625, ((0, 8),), jnp.float32),
    }


def lagged_apply(hidden_states, column_block):
    vectors = column_block.astype(jnp.bfloat16)
    projected = jnp.dot(hidden_states, vectors, preferred_element_type=jnp.float32)
    padding = jnp.zeros((LAG, projected.shape[1]), jnp.float32)
    ahead = jnp.concatenate([projected[LAG:], padding], axis=0)
    behind = jnp.concatenate([padding, projected[:-LAG]], axis=0)
    lagged = (ahead + behind).astype(jnp.bfloat16)
    backward = lax.dot_general(hidden_states, lagged, (((0,), (0,)), ((), ())), preferred_element_type=jnp.float32)
    return backward * (0.5 / math.sqrt(TOKENS - LAG))

def reference(hidden_states, current_block, directions):
    highest = lax.Precision.HIGHEST
    image_x = lagged_apply(hidden_states, current_block)
    rayleigh = jnp.dot(current_block.T, image_x, precision=highest)
    residual = image_x - jnp.dot(current_block, rayleigh, precision=highest)
    lengths = lax.optimization_barrier(jnp.sum(residual * residual, axis=0, keepdims=True))
    unit_residual = residual * lax.rsqrt(lengths + 1e-06)
    image_r = lagged_apply(hidden_states, unit_residual)
    image_p = lagged_apply(hidden_states, directions)
    block_image = jnp.concatenate([image_x, image_r, image_p], axis=1)
    search = jnp.concatenate([current_block, unit_residual, directions], axis=1)
    gram_image = jnp.dot(search.T, block_image, precision=highest)
    gram_search = jnp.dot(search.T, search, precision=highest)
    return (block_image, gram_image, gram_search)
```

```python
import math

import jax
import jax.numpy as jnp
from jax import lax
from jax.sharding import PartitionSpec as P

LAG = 256
SMALL = 2.0**-20
HIGHEST = lax.Precision.HIGHEST


def exchange(value, axis):
    return lax.all_to_all(value, axis, 0, 0, tiled=True)


def scattered_sum(value, axis):
    return jnp.sum(exchange(value, axis).astype(jnp.float32), axis=0)


def gathered(value, axis):
    return exchange(jnp.broadcast_to(value, (lax.axis_size(axis),) + value.shape), axis)


def rows_dot(a, b, **kwargs):
    return lax.dot_general(a, b, (((1,), (1,)), ((), ())), preferred_element_type=jnp.float32, **kwargs)


def local(hidden_states, current_block, directions):
    tokens, features = hidden_states.shape
    cols = current_block.shape[1]
    feat, tok = lax.axis_size("feat"), lax.axis_size("tok")
    factor = 0.5 / math.sqrt(tokens * tok - LAG)
    half = jnp.bfloat16

    up = [(i, i + 1) for i in range(tok - 1)]
    down = [(i + 1, i) for i in range(tok - 1)]
    behind = lax.ppermute(hidden_states[tokens - LAG :], "tok", up)
    ahead = lax.ppermute(hidden_states[:LAG], "tok", down)
    x, p = current_block.T, directions.T

    def project(vectors):
        pieces = [rows_dot(vectors, part) for part in (behind, hidden_states, ahead)]
        return jnp.concatenate(pieces, axis=1)

    def lagged(projected):
        return projected[:, 2 * LAG :] + projected[:, : tokens]

    def backward(lagged_rows):
        return lax.dot_general(
            lagged_rows, hidden_states, (((1,), (0,)), ((), ())), preferred_element_type=jnp.float32
        )

    side = lax.psum(
        jnp.concatenate(
            [
                project(p.astype(half)),
                rows_dot(p, jnp.concatenate([x, p]), precision=HIGHEST),
                rows_dot(x, x, precision=HIGHEST),
            ],
            axis=1,
        ),
        "feat",
    )

    part = lagged(project(x.astype(half)))
    own = scattered_sum(part.reshape(feat, cols // feat, tokens), "feat").astype(half)
    lag_x = gathered(own, "feat").reshape(cols, tokens)
    own = scattered_sum(backward(lag_x).reshape(tok, cols // tok, features), "tok") * factor
    image_x = gathered(own, "tok").reshape(cols, features)

    both = rows_dot(image_x, jnp.concatenate([x, p]), precision=HIGHEST)
    both = jnp.sum(gathered(both, "feat"), axis=0)
    rayleigh_t, image_x_p = both[:, :cols], both[:, cols:]
    residual = (image_x - jnp.dot(rayleigh_t, x, precision=HIGHEST)) * SMALL

    width = tokens + 2 * LAG
    part = jnp.concatenate(
        [
            project(residual.astype(half)),
            rows_dot(residual, jnp.concatenate([x, residual, p]), precision=HIGHEST),
        ],
        axis=1,
    )
    own = scattered_sum(part.reshape(feat, cols // feat, part.shape[1]), "feat")
    high = own.astype(half)
    low = (own[:, width:] - high[:, width:].astype(jnp.float32)).astype(half)
    everything = gathered(jnp.concatenate([high, low], axis=1), "feat").reshape(cols, -1)
    proj_r = everything[:, :width]
    inner = everything[:, width:].astype(jnp.float32)
    inner = inner[:, : 3 * cols] + inner[:, 3 * cols :]
    r_x, r_r, r_p = (inner[:, i * cols : (i + 1) * cols] for i in range(3))

    proj_p = side[:, :width]
    lag_r = lagged(proj_r.astype(jnp.float32)).astype(half)
    lag_p = lagged(proj_p).astype(half)
    mid_r = proj_r[:, LAG : LAG + tokens]
    mid_p = proj_p[:, LAG : LAG + tokens].astype(half)
    image = backward(jnp.concatenate([lag_r, lag_p]))
    cross = rows_dot(jnp.concatenate([mid_r, mid_p]), jnp.concatenate([lag_r, lag_p]))
    part = jnp.concatenate(
        [
            image[:cols].reshape(tok, -1),
            image[cols:].reshape(tok, -1),
            cross[:cols, :cols].reshape(tok, -1),
            cross[cols:, :cols].reshape(tok, -1),
            cross[cols:, cols:].reshape(tok, -1),
        ],
        axis=1,
    )
    own = scattered_sum(part[:, None, :], "tok") * factor
    total = gathered(own, "tok")[:, 0, :]
    sizes = [cols * features // tok] * 2 + [cols * cols // tok] * 3
    ends = [sum(sizes[: i + 1]) for i in range(5)]
    image_r, image_p = (total[:, e - s : e].reshape(cols, features) for e, s in zip(ends[:2], sizes[:2]))
    c_rr, c_pr, c_pp = (total[:, e - s : e].reshape(cols, cols) for e, s in zip(ends[2:], sizes[2:]))

    lengths = jnp.sum(r_r * jnp.eye(cols, dtype=jnp.float32), axis=1, keepdims=True)
    scale = lax.rsqrt(lengths * (1.0 / SMALL**2) + 1e-06) * (1.0 / SMALL)
    across = scale.T

    block_image = jnp.concatenate([image_x, image_r * scale, image_p])
    u_x, u_p = r_x * scale, r_p * scale
    u_u = r_r * scale * across
    u_image_x = (r_r * (1.0 / SMALL) + jnp.dot(r_x, rayleigh_t.T, precision=HIGHEST)) * scale
    p_image_u = c_pr * across
    gram_image = jnp.concatenate(
        [
            jnp.concatenate([rayleigh_t.T, u_image_x.T, image_x_p], axis=1),
            jnp.concatenate([u_image_x, c_rr * scale * across, p_image_u.T], axis=1),
            jnp.concatenate([image_x_p.T, p_image_u, c_pp], axis=1),
        ]
    )
    p_x, p_p, x_x = (side[:, width + i * cols : width + (i + 1) * cols] for i in range(3))
    gram_search = jnp.concatenate(
        [
            jnp.concatenate([x_x, u_x.T, p_x.T], axis=1),
            jnp.concatenate([u_x, u_u, u_p], axis=1),
            jnp.concatenate([p_x, u_p.T, p_p], axis=1),
        ]
    )
    return (block_image.T, gram_image, gram_search)


def solution(mesh):
    return jax.shard_map(
        local,
        mesh=mesh,
        in_specs=(P("tok", "feat"), P("feat", None), P("feat", None)),
        out_specs=(P("feat", None), P(), P()),
        check_vma=False,
    )
```

```python
import math

import jax
import jax.numpy as jnp
from jax import lax
from jax.sharding import PartitionSpec as P

LAG = 256
SMALL = 2.0**-20
HIGHEST = lax.Precision.HIGHEST


def exchange(value, axis):
    return lax.all_to_all(value, axis, 0, 0, tiled=True)


def scattered_sum(value, axis):
    return jnp.sum(exchange(value, axis).astype(jnp.float32), axis=0)


def gathered(value, axis):
    return exchange(jnp.broadcast_to(value, (lax.axis_size(axis),) + value.shape), axis)


def rows_dot(a, b, **kwargs):
    return lax.dot_general(a, b, (((1,), (1,)), ((), ())), preferred_element_type=jnp.float32, **kwargs)


def pair(value):
    high = value.astype(jnp.bfloat16)
    return jnp.concatenate([high, (value - high.astype(jnp.float32)).astype(jnp.bfloat16)], axis=1)


def joined(value):
    value = value.astype(jnp.float32)
    middle = value.shape[1] // 2
    return value[:, :middle] + value[:, middle:]


def local(hidden_states, current_block, directions):
    tokens, features = hidden_states.shape
    cols = current_block.shape[1]
    feat, tok = lax.axis_size("feat"), lax.axis_size("tok")
    factor = 0.5 / math.sqrt(tokens * tok - LAG)
    half = jnp.bfloat16

    up = [(i, i + 1) for i in range(tok - 1)]
    down = [(i + 1, i) for i in range(tok - 1)]
    behind = lax.ppermute(hidden_states[tokens - LAG :], "tok", up)
    ahead = lax.ppermute(hidden_states[:LAG], "tok", down)
    x, p = current_block.T, directions.T
    width = tokens + 2 * LAG

    def project(vectors):
        pieces = [rows_dot(vectors, part).astype(half) for part in (behind, hidden_states, ahead)]
        return jnp.concatenate(pieces, axis=1)

    def lagged(projected):
        projected = projected.astype(jnp.float32)
        return (projected[:, 2 * LAG :] + projected[:, :tokens]).astype(half)

    def middle(projected):
        return projected[:, LAG : LAG + tokens]

    def backward(lagged_rows):
        return lax.dot_general(
            lagged_rows, hidden_states, (((1,), (0,)), ((), ())), preferred_element_type=jnp.float32
        )

    def inner(a, b):
        return rows_dot(a, b, precision=HIGHEST)

    def times(a, b):
        return jnp.dot(a, b, precision=HIGHEST)

    part = project(jnp.concatenate([x.astype(half), p.astype(half)]))
    zero = jnp.zeros((cols, cols), jnp.float32)
    products = jnp.concatenate(
        [jnp.concatenate([inner(x, x), inner(p, x)]), jnp.concatenate([zero, inner(p, p)])], axis=1
    )
    part = jnp.concatenate([part, pair(products)], axis=1)
    own = scattered_sum(part.reshape(feat, 2 * cols // feat, part.shape[1]), "feat")
    own = jnp.concatenate([own[:, :width].astype(half), pair(joined(own[:, width:]))], axis=1)
    known = gathered(own, "feat").reshape(2 * cols, -1)
    proj_x, proj_p = known[:cols, :width], known[cols:, :width]
    lag_x, lag_p = lagged(proj_x), lagged(proj_p)

    part = jnp.concatenate(
        [backward(lag_x).reshape(tok, -1), rows_dot(lag_x, middle(proj_x)).reshape(tok, -1)], axis=1
    )
    own = scattered_sum(part[:, None, :], "tok") * factor
    total = gathered(own, "tok")[:, 0, :]
    split = cols * features // tok
    image_x = total[:, :split].reshape(cols, features)
    estimate = total[:, split:].reshape(cols, cols)
    residual = (image_x - times(estimate, x)) * SMALL

    part = project(residual.astype(half))
    products = jnp.concatenate(
        [inner(residual, x), inner(residual, p), inner(residual, residual), inner(image_x, x), inner(image_x, p)],
        axis=1,
    )
    part = jnp.concatenate([part, pair(products)], axis=1)
    own = scattered_sum(part.reshape(feat, cols // feat, part.shape[1]), "feat")
    products = joined(own[:, width:])
    first = lax.axis_index("feat") * (cols // feat)
    lacks = (products[:, 3 * cols : 4 * cols] - lax.dynamic_slice_in_dim(estimate, first, cols // feat)) * SMALL
    proj_r = own[:, :width] - jnp.dot(lacks.astype(half), proj_x, preferred_element_type=jnp.float32)
    own = jnp.concatenate([proj_r.astype(half), pair(products)], axis=1)
    found = gathered(own, "feat").reshape(cols, -1)
    proj_r = found[:, :width]
    lag_r = lagged(proj_r)

    part = jnp.concatenate(
        [
            backward(lag_r).astype(half).reshape(tok, -1),
            backward(lag_p).astype(half).reshape(tok, -1),
            pair(rows_dot(middle(proj_r), lag_r).reshape(tok, -1)),
            pair(rows_dot(middle(proj_p), lag_r).reshape(tok, -1)),
            pair(rows_dot(middle(proj_p), lag_p).reshape(tok, -1)),
        ],
        axis=1,
    )
    own = scattered_sum(part[:, None, :], "tok") * factor
    images, own = own[:, : 2 * split].astype(half), own[:, 2 * split :]
    each = cols * cols // tok
    own = [images] + [pair(joined(own[:, 2 * i * each : 2 * (i + 1) * each])) for i in range(3)]
    total = gathered(jnp.concatenate(own, axis=1), "tok")[:, 0, :]
    image_r, image_p = (
        total[:, i * split : (i + 1) * split].reshape(cols, features).astype(jnp.float32) for i in range(2)
    )
    c_rr, c_pr, c_pp = (
        joined(total[:, 2 * (split + i * each) : 2 * (split + (i + 1) * each)]).reshape(cols, cols) for i in range(3)
    )

    products = joined(found[:, width:])
    r_x, r_p, r_r, rayleigh_t, image_x_p = (products[:, i * cols : (i + 1) * cols] for i in range(5))
    products = joined(known[:, width:])
    x_x, p_x, p_p = products[:cols, :cols], products[cols:, :cols], products[cols:, cols:]
    lacks = (rayleigh_t - estimate) * SMALL
    shift = times(lacks, r_x.T)
    r_r = r_r - shift - shift.T + times(times(lacks, x_x), lacks.T)
    r_x = r_x - times(lacks, x_x)
    r_p = r_p - times(lacks, p_x.T)

    lengths = jnp.sum(r_r * jnp.eye(cols, dtype=jnp.float32), axis=1, keepdims=True)
    scale = lax.rsqrt(lengths * (1.0 / SMALL**2) + 1e-06) * (1.0 / SMALL)
    across = scale.T

    block_image = jnp.concatenate([image_x, image_r * scale, image_p])
    u_x, u_p = r_x * scale, r_p * scale
    u_u = r_r * scale * across
    u_image_x = (r_r * (1.0 / SMALL) + times(r_x, rayleigh_t.T)) * scale
    p_image_u = c_pr * across
    gram_image = jnp.concatenate(
        [
            jnp.concatenate([rayleigh_t.T, u_image_x.T, image_x_p], axis=1),
            jnp.concatenate([u_image_x, c_rr * scale * across, p_image_u.T], axis=1),
            jnp.concatenate([image_x_p.T, p_image_u, c_pp], axis=1),
        ]
    )
    gram_search = jnp.concatenate(
        [
            jnp.concatenate([x_x, u_x.T, p_x.T], axis=1),
            jnp.concatenate([u_x, u_u, u_p], axis=1),
            jnp.concatenate([p_x, u_p.T, p_p], axis=1),
        ]
    )
    return (block_image.T, gram_image, gram_search)


def solution(mesh):
    return jax.shard_map(
        local,
        mesh=mesh,
        in_specs=(P("tok", "feat"), P("feat", None), P("feat", None)),
        out_specs=(P("feat", None), P(), P()),
        check_vma=False,
    )
```

```python
import functools
import math

import jax
import jax.numpy as jnp
from jax import lax
from jax.experimental import pallas as pl
from jax.experimental.pallas import tpu as pltpu
from jax.sharding import PartitionSpec as P

LAG = 256
SMALL = 2.0**-20
LANES = 128
HIGHEST = lax.Precision.HIGHEST
HALF = jnp.bfloat16
FLOAT = jnp.float32


def padded(size):
    return -(-size // LANES) * LANES


def exchange(value, axis):
    return lax.all_to_all(value, axis, 0, 0, tiled=True)


def kernel_call(body, outputs, *operands):
    many = isinstance(outputs, list)
    spec = pl.BlockSpec(memory_space=pltpu.VMEM)
    return pl.pallas_call(
        body,
        out_shape=outputs,
        in_specs=[spec] * len(operands),
        out_specs=[spec] * len(outputs) if many else spec,
        compiler_params=pltpu.CompilerParams(vmem_limit_bytes=48 * 2**20),
    )(*operands)


def shape(dims, dtype):
    return jax.ShapeDtypeStruct(dims, dtype)


def rows_dot(a, b, precision=None):
    return lax.dot_general(a, b, (((1,), (1,)), ((), ())), preferred_element_type=FLOAT, precision=precision)


def exact(a, b):
    return rows_dot(a, b, HIGHEST)


def times(a, b):
    return jnp.dot(a, b, precision=HIGHEST, preferred_element_type=FLOAT)


def high_low(value):
    high = value.astype(HALF)
    return high, (value - high.astype(FLOAT)).astype(HALF)


def joined(value):
    value = value.astype(FLOAT)
    middle = value.shape[1] // 2
    return value[:, :middle] + value[:, middle:]


def project_own(vectors, hidden, out):
    whole = hidden.shape[0] // LANES * LANES
    out[:, LAG : LAG + whole] = rows_dot(vectors, hidden[:whole]).astype(HALF)


def project_edges(vectors, hidden_tail, behind, ahead, out, tokens):
    whole = tokens // LANES * LANES
    width = tokens + 2 * LAG
    rest = tokens - whole
    fill = (LANES - rest) % LANES
    rows = vectors.shape[0]
    out[:, :LAG] = rows_dot(vectors, behind[...]).astype(HALF)
    if rest:
        tile = jnp.concatenate([hidden_tail, ahead[:fill]])
        out[:, LAG + whole : LAG + whole + LANES] = rows_dot(vectors, tile).astype(HALF)
    last = rows_dot(vectors, ahead[fill:]).astype(HALF)
    spare = padded(width) - width
    if spare:
        last = jnp.concatenate([last, jnp.zeros((rows, spare), HALF)], axis=1)
    out[:, LAG + whole + rest + fill : padded(width)] = last


def start_kernel(x, p, hidden, out):
    cols, wide = x.shape[0], out.shape[1] - 4 * x.shape[0]
    both = jnp.concatenate([x[...], p[...]])
    project_own(both.astype(HALF), hidden, out)
    high, low = high_low(exact(both, both))
    out[:, wide : wide + 2 * cols] = high
    out[:, wide + 2 * cols :] = low


def edge_kernel(tokens, x, p, tail, behind, ahead, start, out):
    out[...] = start[...]
    both = jnp.concatenate([x[...], p[...]]).astype(HALF)
    project_edges(both, tail[...], behind, ahead, out, tokens)


def known_kernel(wide, received, out):
    total = jnp.sum(received[...].astype(FLOAT), axis=0)
    high, low = high_low(joined(total[:, wide:]))
    total = jnp.concatenate([total[:, :wide].astype(HALF), high, low], axis=1)
    out[...] = jnp.broadcast_to(total, out.shape)


def shifted(projected, tokens):
    return [projected[:, 2 * LAG : 2 * LAG + tokens], projected[:, :tokens]]


def first_kernel(known, hidden, out):
    tokens, features = hidden.shape
    cols = out.shape[0]
    projected = known[:cols]
    halves = jnp.concatenate(shifted(projected, tokens))
    image = jnp.dot(halves, hidden[...], preferred_element_type=FLOAT)
    out[:, :features] = image[:cols] + image[cols:]
    cross = rows_dot(halves, projected[:, LAG : LAG + tokens])
    out[:, features:] = cross[:cols] + cross[cols:]


def residual_kernel(total, x, p, hidden, behind, ahead, out):
    tokens, features = hidden.shape
    cols = x.shape[0]
    image = total[:, :features]
    residual = (image - times(total[:, features:], x[...])) * SMALL
    rounded = residual.astype(HALF)
    project_own(rounded, hidden, out)
    project_edges(rounded, hidden[tokens // LANES * LANES :], behind, ahead, out, tokens)
    both = jnp.concatenate([x[...], p[...]])
    products = exact(jnp.concatenate([residual, image]), both)
    own = exact(jnp.concatenate([residual, residual]), residual)[:cols]
    own = jnp.concatenate([own, jnp.zeros_like(own)], axis=1)
    at = padded(tokens + 2 * LAG)
    for value in (products[:cols], products[cols:], own):
        high, low = high_low(value)
        out[:, at : at + 2 * cols] = high
        out[:, at + 6 * cols : at + 8 * cols] = low
        at += 2 * cols


def found_kernel(wide, where, received, estimate, known, out):
    rows = received.shape[1]
    cols = estimate.shape[0]
    total = jnp.sum(received[...].astype(FLOAT), axis=0)
    products = joined(total[:, wide:])
    first = pl.multiple_of(where[0] * rows, rows)
    lacks = (products[:, 2 * cols : 3 * cols] - estimate[pl.ds(first, rows), :]) * SMALL
    lacks = jnp.concatenate([lacks, jnp.zeros_like(lacks)]).astype(HALF)
    shift = jnp.dot(lacks, known[:cols, :wide], preferred_element_type=FLOAT)[:rows]
    high, low = high_low(products)
    total = jnp.concatenate([(total[:, :wide] - shift).astype(HALF), high, low], axis=1)
    out[...] = jnp.broadcast_to(total, out.shape)


def image_kernel(blocks, found, known, hidden, out):
    tokens, features = hidden.shape
    cols = found.shape[0]
    span = features // blocks
    proj_r, proj_p = found[:, : tokens + 2 * LAG], known[cols:, : tokens + 2 * LAG]
    halves = jnp.concatenate(shifted(proj_r, tokens) + shifted(proj_p, tokens))
    middles = jnp.concatenate([proj_r[:, LAG : LAG + tokens], proj_p[:, LAG : LAG + tokens]])
    image = jnp.dot(halves, hidden[...], preferred_element_type=FLOAT)
    cross = rows_dot(halves, middles)

    def summed(value):
        return jnp.concatenate(
            [value[:cols] + value[cols : 2 * cols], value[2 * cols : 3 * cols] + value[3 * cols :]]
        )

    image, cross = summed(image), summed(cross)
    high = cross.astype(HALF).astype(FLOAT)
    low = cross - high
    left = lax.broadcasted_iota(jnp.int32, cross.shape, 1) < cols
    pieces = [
        jnp.where(left, high, pltpu.roll(low, cols, 1)),
        jnp.where(left, pltpu.roll(high, cols, 1), low),
    ]
    groups = 2 * cols // 8
    for g in range(groups):
        for b in range(blocks):
            out[g * blocks + b, :, :span] = image[8 * g : 8 * g + 8, b * span : (b + 1) * span].astype(HALF)
    for k in range(out.shape[0]):
        if k < 2 * groups:
            g = k % groups
            out[k, :, span:] = pieces[k // groups][8 * g : 8 * g + 8].astype(HALF)
        else:
            out[k, :, span:] = jnp.zeros((8, 2 * cols), HALF)


def total_kernel(factor, cols, received, out):
    span = received.shape[2] - 2 * cols
    total = jnp.sum(received[...].astype(FLOAT), axis=0) * factor
    cross = total[:, span:]
    cross = cross + pltpu.roll(cross, cols, 1)
    high = cross.astype(HALF).astype(FLOAT)
    left = lax.broadcasted_iota(jnp.int32, cross.shape, 1) < cols
    cross = jnp.where(left, high, cross - high)
    total = jnp.concatenate([total[:, :span], cross], axis=1).astype(HALF)
    out[...] = jnp.broadcast_to(total, out.shape)


def last_kernel(blocks, gathered, first_total, scale, across, top, u_image_x, p_image_x, images, gram):
    cols = scale.shape[0]
    features = images.shape[1]
    span = features // blocks
    groups = cols // 8
    images[:cols] = first_total[:, :features]
    for g in range(groups):
        for b in range(blocks):
            at = slice(b * span, (b + 1) * span)
            rows = slice(cols + 8 * g, cols + 8 * g + 8)
            images[rows, at] = gathered[g * blocks + b, :, :span].astype(FLOAT) * scale[8 * g : 8 * g + 8]
            rows = slice(2 * cols + 8 * g, 2 * cols + 8 * g + 8)
            images[rows, at] = gathered[(groups + g) * blocks + b, :, :span].astype(FLOAT)

    def piece(first):
        value = jnp.concatenate([gathered[k, :, span:].astype(FLOAT) for k in range(first, first + groups)])
        return (value + pltpu.roll(value, cols, 1))[:, :cols]

    rr, pr, rp, pp = (piece(i * groups) for i in range(4))
    gram[:cols] = top[...]
    gram[cols : 2 * cols, :cols] = u_image_x[...]
    gram[cols : 2 * cols, cols : 2 * cols] = rr * scale[...] * across[...]
    gram[cols : 2 * cols, 2 * cols :] = rp * scale[...]
    gram[2 * cols :, :cols] = p_image_x[...]
    gram[2 * cols :, cols : 2 * cols] = pr * across[...]
    gram[2 * cols :, 2 * cols :] = pp


def local(hidden_states, current_block, directions):
    tokens, features = hidden_states.shape
    cols = current_block.shape[1]
    feat, tok = lax.axis_size("feat"), lax.axis_size("tok")
    factor = 0.5 / math.sqrt(tokens * tok - LAG)
    wide = padded(tokens + 2 * LAG)
    blocks = tok * 8 // (2 * cols)

    up = [(i, i + 1) for i in range(tok - 1)]
    down = [(i + 1, i) for i in range(tok - 1)]
    behind = lax.ppermute(hidden_states[tokens - LAG :], "tok", up)
    ahead = lax.ppermute(hidden_states[:LAG], "tok", down)
    x, p = current_block.T, directions.T

    total = wide + 4 * cols
    part = kernel_call(start_kernel, shape((2 * cols, total), HALF), x, p, hidden_states)
    tail = hidden_states[tokens // LANES * LANES :]
    part = kernel_call(
        functools.partial(edge_kernel, tokens), shape((2 * cols, total), HALF), x, p, tail, behind, ahead, part
    )
    blocked = shape((feat, 2 * cols // feat, total), HALF)
    part = exchange(part.reshape(blocked.shape), "feat")
    part = kernel_call(functools.partial(known_kernel, wide), blocked, part)
    known = exchange(part, "feat").reshape(2 * cols, total)

    part = kernel_call(first_kernel, shape((cols, features + cols), FLOAT), known, hidden_states)
    part = exchange(part.reshape(tok, 1, -1), "tok")
    part = jnp.sum(part, axis=0) * factor
    part = exchange(jnp.broadcast_to(part, (tok,) + part.shape), "tok")
    first_total = part.reshape(cols, features + cols)
    estimate = first_total[:, features:]

    total = wide + 12 * cols
    part = kernel_call(
        residual_kernel, shape((cols, total), HALF), first_total, x, p, hidden_states, behind, ahead
    )
    blocked = shape((feat, cols // feat, total), HALF)
    part = exchange(part.reshape(blocked.shape), "feat")
    where = lax.axis_index("feat").astype(jnp.int32).reshape(1)
    vmem = pl.BlockSpec(memory_space=pltpu.VMEM)
    part = pl.pallas_call(
        functools.partial(found_kernel, wide),
        out_shape=blocked,
        in_specs=[pl.BlockSpec(memory_space=pltpu.SMEM), vmem, vmem, vmem],
        out_specs=vmem,
        compiler_params=pltpu.CompilerParams(vmem_limit_bytes=48 * 2**20),
    )(where, part, estimate, known)
    found = exchange(part, "feat").reshape(cols, total)

    blocked = shape((tok, 8, features // blocks + 2 * cols), HALF)
    part = kernel_call(functools.partial(image_kernel, blocks), blocked, found, known, hidden_states)
    part = exchange(part, "tok")
    part = kernel_call(functools.partial(total_kernel, factor, cols), blocked, part)
    gathered = exchange(part, "tok")

    products = joined(found[:, wide:])
    r_x, r_p, rayleigh_t, image_x_p, r_r = (products[:, i * cols : (i + 1) * cols] for i in range(5))
    products = joined(known[:, wide:])
    x_x, p_x, p_p = products[:cols, :cols], products[cols:, :cols], products[cols:, cols:]
    lacks = (rayleigh_t - estimate) * SMALL
    shift = times(lacks, r_x.T)
    r_r = r_r - shift - shift.T + times(times(lacks, x_x), lacks.T)
    r_x = r_x - times(lacks, x_x)
    r_p = r_p - times(lacks, p_x.T)

    lengths = jnp.sum(r_r * jnp.eye(cols, dtype=FLOAT), axis=1, keepdims=True)
    scale = lax.rsqrt(lengths * (1.0 / SMALL**2) + 1e-06) * (1.0 / SMALL)
    across = scale.T
    u_x, u_p = r_x * scale, r_p * scale
    u_u = r_r * scale * across
    u_image_x = (r_r * (1.0 / SMALL) + times(r_x, rayleigh_t.T)) * scale
    top = jnp.concatenate([rayleigh_t.T, u_image_x.T, image_x_p], axis=1)
    gram_search = jnp.concatenate(
        [
            jnp.concatenate([x_x, u_x.T, p_x.T], axis=1),
            jnp.concatenate([u_x, u_u, u_p], axis=1),
            jnp.concatenate([p_x, u_p.T, p_p], axis=1),
        ]
    )
    images, gram_image = kernel_call(
        functools.partial(last_kernel, blocks),
        [shape((3 * cols, features), FLOAT), shape((3 * cols, 3 * cols), FLOAT)],
        gathered,
        first_total,
        scale,
        across,
        top,
        u_image_x,
        image_x_p.T,
    )
    return (images.T, gram_image, gram_search)


def solution(mesh):
    return jax.shard_map(
        local,
        mesh=mesh,
        in_specs=(P("tok", "feat"), P("feat", None), P("feat", None)),
        out_specs=(P("feat", None), P(), P()),
        check_vma=False,
    )
```

```python
import functools
import math

import jax
import jax.numpy as jnp
from jax import lax
from jax.experimental import pallas as pl
from jax.experimental.pallas import tpu as pltpu
from jax.sharding import PartitionSpec as P

LAG = 256
SMALL = 2.0**-20
LANES = 128
HIGHEST = lax.Precision.HIGHEST
HALF = jnp.bfloat16
FLOAT = jnp.float32


def padded(size):
    return -(-size // LANES) * LANES


def exchange(value, axis):
    return lax.all_to_all(value, axis, 0, 0, tiled=True)


def kernel_call(body, outputs, *operands):
    many = isinstance(outputs, list)
    spec = pl.BlockSpec(memory_space=pltpu.VMEM)
    return pl.pallas_call(
        body,
        out_shape=outputs,
        in_specs=[spec] * len(operands),
        out_specs=[spec] * len(outputs) if many else spec,
        compiler_params=pltpu.CompilerParams(vmem_limit_bytes=16 * 2**20),
    )(*operands)


def shape(dims, dtype):
    return jax.ShapeDtypeStruct(dims, dtype)


def rows_dot(a, b, precision=None):
    return lax.dot_general(a, b, (((1,), (1,)), ((), ())), preferred_element_type=FLOAT, precision=precision)


def exact(a, b):
    return rows_dot(a, b, HIGHEST)


def times(a, b):
    return jnp.dot(a, b, precision=HIGHEST, preferred_element_type=FLOAT)


def high_low(value):
    high = value.astype(HALF)
    return high, (value - high.astype(FLOAT)).astype(HALF)


def joined(value):
    value = value.astype(FLOAT)
    middle = value.shape[1] // 2
    return value[:, :middle] + value[:, middle:]


def project_own(vectors, hidden, out):
    whole = hidden.shape[0] // LANES * LANES
    out[:, :whole] = rows_dot(vectors, hidden[:whole]).astype(HALF)


def project_edge(vectors, tail, ahead):
    rows, rest = vectors.shape[0], tail.shape[0]
    value = rows_dot(vectors, jnp.concatenate([tail, ahead[...]])).astype(HALF)
    spare = padded(rest + LAG) - rest - LAG
    if spare:
        value = jnp.concatenate([value, jnp.zeros((rows, spare), HALF)], axis=1)
    return value


def start_kernel(x, p, hidden, out):
    cols = x.shape[0]
    wide = out.shape[1] - 4 * cols
    both = jnp.concatenate([x[...], p[...]])
    project_own(both.astype(HALF), hidden, out)
    high, low = high_low(exact(both, both))
    out[:, wide : wide + 2 * cols] = high
    out[:, wide + 2 * cols :] = low


def edge_kernel(whole, x, p, tail, ahead, start, out):
    wide = out.shape[1] - 4 * x.shape[0]
    out[:, :whole] = start[:, :whole]
    out[:, wide:] = start[:, wide:]
    both = jnp.concatenate([x[...], p[...]]).astype(HALF)
    out[:, whole:wide] = project_edge(both, tail[...], ahead)


def known_kernel(wide, received, out):
    total = jnp.sum(received[...].astype(FLOAT), axis=0)
    high, low = high_low(joined(total[:, wide:]))
    total = jnp.concatenate([total[:, :wide].astype(HALF), high, low], axis=1)
    out[...] = jnp.broadcast_to(total, out.shape)


def lag_image(projected, hidden, ahead):
    tokens = hidden.shape[0]
    cut = tokens // LANES * LANES - LAG
    here, later = projected[:, :tokens], projected[:, LAG : LAG + tokens]
    edge = jnp.concatenate([hidden[cut + LAG :], ahead[...]])
    image = jnp.dot(later, hidden[...], preferred_element_type=FLOAT)
    image += jnp.dot(here[:, :cut], hidden[LAG : LAG + cut], preferred_element_type=FLOAT)
    image += jnp.dot(here[:, cut:], edge, preferred_element_type=FLOAT)
    return image, rows_dot(later, here) + rows_dot(here, later)


def first_kernel(known, hidden, ahead, out):
    features = hidden.shape[1]
    image, cross = lag_image(known[: out.shape[0]], hidden, ahead)
    out[:, :features] = image
    out[:, features:] = cross


def residual_kernel(feat, total, x, p, hidden, ahead, out):
    tokens, features = hidden.shape
    cols = x.shape[0]
    whole, at = tokens // LANES * LANES, padded(tokens + LAG)
    image = total[:, :features]
    residual = (image - times(total[:, features:], x[...])) * SMALL
    rounded = residual.astype(HALF)
    project_own(rounded, hidden, out)
    out[:, whole:at] = project_edge(rounded, hidden[whole:], ahead)
    both = jnp.concatenate([x[...], p[...]])
    products = exact(jnp.concatenate([residual, image]), both)
    share = total[:, features:] * (1.0 / feat)
    lacks = products[cols:] - jnp.concatenate([share, jnp.zeros_like(share)], axis=1)
    own = exact(jnp.concatenate([residual, residual]), residual)[:cols]
    own = jnp.concatenate([own, jnp.zeros_like(own)], axis=1)
    for value in (products[:cols], lacks, own):
        high, low = high_low(value)
        out[:, at : at + 2 * cols] = high
        out[:, at + 6 * cols : at + 8 * cols] = low
        at += 2 * cols


def found_kernel(wide, received, known, out):
    rows = received.shape[1]
    cols = known.shape[0] // 2
    total = jnp.sum(received[...].astype(FLOAT), axis=0)
    products = joined(total[:, wide:])
    lacks = products[:, 2 * cols : 3 * cols] * SMALL
    lacks = jnp.concatenate([lacks, jnp.zeros_like(lacks)]).astype(HALF)
    shift = jnp.dot(lacks, known[:cols, :wide], preferred_element_type=FLOAT)[:rows]
    high, low = high_low(products)
    total = jnp.concatenate([(total[:, :wide] - shift).astype(HALF), high, low], axis=1)
    out[...] = jnp.broadcast_to(total, out.shape)


def side_by_side(first, second):
    cols = first.shape[1] // 2
    left = lax.broadcasted_iota(jnp.int32, first.shape, 1) < cols
    return jnp.where(left, first, pltpu.roll(second, cols, 1))


def image_kernel(blocks, found, known, hidden, ahead, out):
    tokens, features = hidden.shape
    cols = found.shape[0]
    span = features // blocks
    wide = padded(tokens + LAG)
    image, cross = lag_image(jnp.concatenate([found[:, :wide], known[cols:, :wide]]), hidden, ahead)
    high = cross.astype(HALF).astype(FLOAT)
    low = cross - high
    pieces = [side_by_side(high, low), side_by_side(pltpu.roll(high, cols, 1), pltpu.roll(low, cols, 1))]
    groups = 2 * cols // 8
    for g in range(groups):
        for b in range(blocks):
            out[g * blocks + b, :, :span] = image[8 * g : 8 * g + 8, b * span : (b + 1) * span].astype(HALF)
    for k in range(out.shape[0]):
        if k < 2 * groups:
            g = k % groups
            out[k, :, span:] = pieces[k // groups][8 * g : 8 * g + 8].astype(HALF)
        else:
            out[k, :, span:] = jnp.zeros((8, 2 * cols), HALF)


def total_kernel(factor, cols, received, out):
    span = received.shape[2] - 2 * cols
    total = jnp.sum(received[...].astype(FLOAT), axis=0) * factor
    cross = total[:, span:]
    cross = cross + pltpu.roll(cross, cols, 1)
    high = cross.astype(HALF).astype(FLOAT)
    left = lax.broadcasted_iota(jnp.int32, cross.shape, 1) < cols
    cross = jnp.where(left, high, cross - high)
    total = jnp.concatenate([total[:, :span], cross], axis=1).astype(HALF)
    out[...] = jnp.broadcast_to(total, out.shape)


def inner_products(wide, first_total, found, known, search):
    cols = found.shape[0]
    products = joined(found[:, wide:])
    r_x, r_p, lacks, image_x_p, r_r = (products[:, i * cols : (i + 1) * cols] for i in range(5))
    products = joined(known[:, wide:])
    x_x, p_x, p_p = products[:cols, :cols], products[cols:, :cols], products[cols:, cols:]
    rayleigh_t = first_total[:, first_total.shape[1] - cols :] + lacks
    lacks = lacks * SMALL
    lacks_xx = times(lacks, x_x)
    r_r = r_r - exact(lacks, r_x) - exact(r_x, lacks) + exact(lacks_xx, lacks)
    r_x = r_x - lacks_xx
    r_p = r_p - exact(lacks, p_x)
    square = (cols, cols)
    eye = lax.broadcasted_iota(jnp.int32, square, 0) == lax.broadcasted_iota(jnp.int32, square, 1)
    lengths = jnp.where(eye, r_r, 0.0)

    def scaling(lengths):
        return lax.rsqrt(lengths * (1.0 / SMALL**2) + 1e-06) * (1.0 / SMALL)

    scale = scaling(jnp.sum(lengths, axis=1, keepdims=True))
    across = scaling(jnp.sum(lengths, axis=0, keepdims=True))
    u_image_x = (r_r * (1.0 / SMALL) + exact(r_x, rayleigh_t)) * scale
    u_x, u_p = r_x * scale, r_p * scale
    turned = exact(eye.astype(FLOAT), jnp.concatenate([rayleigh_t, u_image_x, image_x_p, u_x, p_x, u_p]))
    turned = [turned[:, i * cols : (i + 1) * cols] for i in range(6)]
    rows = [[x_x, turned[3], turned[4]], [u_x, r_r * scale * across, u_p], [p_x, turned[5], p_p]]
    for i, row in enumerate(rows):
        search[i * cols : (i + 1) * cols] = jnp.concatenate(row, axis=1)
    return scale, across, turned[:3], u_image_x, image_x_p


def last_kernel(blocks, wide, gathered, first_total, found, known, images, gram, search):
    cols = found.shape[0]
    scale, across, turned, u_image_x, image_x_p = inner_products(wide, first_total, found, known, search)
    features = images.shape[1]
    span = features // blocks
    groups = cols // 8
    images[:cols] = first_total[:, :features]
    for g in range(groups):
        for b in range(blocks):
            at = slice(b * span, (b + 1) * span)
            rows = slice(cols + 8 * g, cols + 8 * g + 8)
            images[rows, at] = gathered[g * blocks + b, :, :span].astype(FLOAT) * scale[8 * g : 8 * g + 8]
            rows = slice(2 * cols + 8 * g, 2 * cols + 8 * g + 8)
            images[rows, at] = gathered[(groups + g) * blocks + b, :, :span].astype(FLOAT)

    def piece(first):
        value = jnp.concatenate([gathered[k, :, span:].astype(FLOAT) for k in range(first, first + groups)])
        return (value + pltpu.roll(value, cols, 1))[:, :cols]

    rr, pr, rp, pp = (piece(i * groups) for i in range(4))
    rows = [
        [turned[0], turned[1], image_x_p],
        [u_image_x, rr * scale * across, rp * scale],
        [turned[2], pr * across, pp],
    ]
    for i, row in enumerate(rows):
        gram[i * cols : (i + 1) * cols] = jnp.concatenate(row, axis=1)


def local(hidden_states, current_block, directions):
    tokens, features = hidden_states.shape
    cols = current_block.shape[1]
    feat, tok = lax.axis_size("feat"), lax.axis_size("tok")
    factor = 0.5 / math.sqrt(tokens * tok - LAG)
    whole, wide = tokens // LANES * LANES, padded(tokens + LAG)
    blocks = tok * 8 // (2 * cols)

    ahead = lax.ppermute(hidden_states[:LAG], "tok", [(i + 1, i) for i in range(tok - 1)])
    x, p = current_block.T, directions.T

    total = wide + 4 * cols
    flat = shape((2 * cols, total), HALF)
    part = kernel_call(start_kernel, flat, x, p, hidden_states)
    part = kernel_call(functools.partial(edge_kernel, whole), flat, x, p, hidden_states[whole:], ahead, part)
    blocked = shape((feat, 2 * cols // feat, total), HALF)
    part = exchange(part.reshape(blocked.shape), "feat")
    part = kernel_call(functools.partial(known_kernel, wide), blocked, part)
    known = exchange(part, "feat").reshape(2 * cols, total)

    part = kernel_call(first_kernel, shape((cols, features + cols), FLOAT), known, hidden_states, ahead)
    part = exchange(part.reshape(tok, 1, -1), "tok")
    part = jnp.sum(part, axis=0) * factor
    part = exchange(jnp.broadcast_to(part, (tok,) + part.shape), "tok")
    first_total = part.reshape(cols, features + cols)

    total = wide + 12 * cols
    part = kernel_call(
        functools.partial(residual_kernel, feat), shape((cols, total), HALF), first_total, x, p, hidden_states, ahead
    )
    blocked = shape((feat, cols // feat, total), HALF)
    part = exchange(part.reshape(blocked.shape), "feat")
    part = kernel_call(functools.partial(found_kernel, wide), blocked, part, known)
    found = exchange(part, "feat").reshape(cols, total)

    blocked = shape((tok, 8, features // blocks + 2 * cols), HALF)
    part = kernel_call(functools.partial(image_kernel, blocks), blocked, found, known, hidden_states, ahead)
    part = exchange(part, "tok")
    part = kernel_call(functools.partial(total_kernel, factor, cols), blocked, part)
    gathered = exchange(part, "tok")
    gram = shape((3 * cols, 3 * cols), FLOAT)
    images, gram_image, gram_search = kernel_call(
        functools.partial(last_kernel, blocks, wide),
        [shape((3 * cols, features), FLOAT), gram, gram],
        gathered,
        first_total,
        found,
        known,
    )
    return (images.T, gram_image, gram_search)


def solution(mesh):
    return jax.shard_map(
        local,
        mesh=mesh,
        in_specs=(P("tok", "feat"), P("feat", None), P("feat", None)),
        out_specs=(P("feat", None), P(), P()),
        check_vma=False,
    )
```

```python
import functools
import math

import jax
import jax.numpy as jnp
from jax import lax
from jax.experimental import pallas as pl
from jax.experimental.pallas import tpu as pltpu
from jax.sharding import PartitionSpec as P

LAG = 256
SMALL = 2.0**-20
LANES = 128
HIGHEST = lax.Precision.HIGHEST
HALF = jnp.bfloat16
FLOAT = jnp.float32


def padded(size):
    return -(-size // LANES) * LANES


def exchange(value, axis):
    return lax.all_to_all(value, axis, 0, 0, tiled=True)


def kernel_call(body, outputs, *operands, far=0):
    many = isinstance(outputs, list)
    vmem, hbm = (pl.BlockSpec(memory_space=space) for space in (pltpu.VMEM, pltpu.HBM))
    near, count = len(operands) - far, len(outputs) if many else 1

    def kernel(*refs):
        sources, rest = refs[near : len(operands)], refs[len(operands) :]
        if not far:
            return body(*refs)
        buffers, semaphores = rest[count:-1], rest[-1]
        copies = [
            pltpu.make_async_copy(source, buffer, semaphores.at[i])
            for i, (source, buffer) in enumerate(zip(sources, buffers))
        ]
        for copy in copies:
            copy.start()
        arrived = set()

        def waiting(i):
            def ref():
                if i not in arrived:
                    arrived.add(i)
                    copies[i].wait()
                return buffers[i]

            return ref

        body(*refs[:near], *[waiting(i) for i in range(far)], *rest[:count])

    scratch = [pltpu.VMEM(value.shape, value.dtype) for value in operands[near:]]
    return pl.pallas_call(
        kernel,
        out_shape=outputs,
        in_specs=[vmem] * near + [hbm] * far,
        out_specs=[vmem] * count if many else vmem,
        scratch_shapes=scratch + [pltpu.SemaphoreType.DMA((far,))] if far else [],
        compiler_params=pltpu.CompilerParams(vmem_limit_bytes=16 * 2**20),
    )(*operands)


def shape(dims, dtype):
    return jax.ShapeDtypeStruct(dims, dtype)


def rows_dot(a, b, precision=None):
    return lax.dot_general(a, b, (((1,), (1,)), ((), ())), preferred_element_type=FLOAT, precision=precision)


def exact(a, b):
    return rows_dot(a, b, HIGHEST)


def times(a, b):
    return jnp.dot(a, b, precision=HIGHEST, preferred_element_type=FLOAT)


def high_low(value):
    high = value.astype(HALF)
    return high, (value - high.astype(FLOAT)).astype(HALF)


def joined(value):
    value = value.astype(FLOAT)
    middle = value.shape[1] // 2
    return value[:, :middle] + value[:, middle:]


def project_own(vectors, hidden, out):
    whole = hidden.shape[0] // LANES * LANES
    out[:, :whole] = rows_dot(vectors, hidden[:whole]).astype(HALF)


def project_edge(vectors, tail, ahead):
    rows, rest = vectors.shape[0], tail.shape[0]
    value = rows_dot(vectors, jnp.concatenate([tail, ahead[...]])).astype(HALF)
    spare = padded(rest + LAG) - rest - LAG
    if spare:
        value = jnp.concatenate([value, jnp.zeros((rows, spare), HALF)], axis=1)
    return value


def start_kernel(both, hidden, out, first):
    both = both[...]
    rounded = both.astype(HALF)
    whole = hidden.shape[0] // LANES * LANES
    wide = out.shape[1] - 2 * both.shape[0]
    products = exact(both, both)
    edge = rows_dot(rounded, hidden[:LAG]).astype(HALF)
    first[...] = edge
    out[:, :LAG] = edge
    out[:, LAG:whole] = rows_dot(rounded, hidden[LAG:whole]).astype(HALF)
    rest = hidden.shape[0] - whole
    if rest:
        tail = rows_dot(rounded, jnp.concatenate([hidden[whole:], hidden[: LANES - rest]])).astype(HALF)
        out[:, whole : whole + LANES] = tail
    high, low = high_low(products)
    out[:, wide : wide + high.shape[1]] = high
    out[:, wide + high.shape[1] :] = low


def edge_kernel(tokens, start, ahead, out):
    rows, whole = start.shape[0], tokens // LANES * LANES
    wide = padded(tokens + LAG)
    out[:, :whole] = start[:, :whole]
    out[:, wide:] = start[:, wide:]
    pieces = [start[:, whole : whole + LANES][:, : tokens - whole]] if tokens > whole else []
    pieces.append(ahead[...])
    if wide > tokens + LAG:
        pieces.append(jnp.zeros((rows, wide - tokens - LAG), HALF))
    out[:, whole:wide] = jnp.concatenate(pieces, axis=1)


def known_kernel(wide, received, out):
    total = jnp.sum(received[...].astype(FLOAT), axis=0)
    high, low = high_low(joined(total[:, wide:]))
    total = jnp.concatenate([total[:, :wide].astype(HALF), high, low], axis=1)
    out[...] = jnp.broadcast_to(total, out.shape)


def lag_image(projected, hidden, ahead):
    tokens = hidden.shape[0]
    cut = tokens // LANES * LANES - LAG
    here, later = projected[:, :tokens], projected[:, LAG : LAG + tokens]
    image = jnp.dot(later, hidden[...], preferred_element_type=FLOAT)
    image += jnp.dot(here[:, :cut], hidden[LAG : LAG + cut], preferred_element_type=FLOAT)
    cross = rows_dot(later, here) + rows_dot(here, later)
    edge = jnp.concatenate([hidden[cut + LAG :], ahead()[...]])
    image += jnp.dot(here[:, cut:], edge, preferred_element_type=FLOAT)
    return image, cross


def first_kernel(known, hidden, ahead, out):
    features = hidden.shape[1]
    image, cross = lag_image(known[: out.shape[0]], hidden, ahead)
    out[:, :features] = image
    out[:, features:] = cross


def residual_kernel(feat, total, hidden, both, ahead, out):
    tokens, features = hidden.shape
    cols = total.shape[0]
    whole, at = tokens // LANES * LANES, padded(tokens + LAG)
    image = total[:, :features]
    residual = (image - times(total[:, features:], both[:cols])) * SMALL
    rounded = residual.astype(HALF)
    project_own(rounded, hidden, out)
    products = exact(jnp.concatenate([residual, image]), both[...])
    own = exact(jnp.concatenate([residual, residual]), residual)[:cols]
    own = jnp.concatenate([own, jnp.zeros_like(own)], axis=1)
    out[:, whole:at] = project_edge(rounded, hidden[whole:], ahead())
    share = total[:, features:] * (1.0 / feat)
    lacks = products[cols:] - jnp.concatenate([share, jnp.zeros_like(share)], axis=1)
    for value in (products[:cols], lacks, own):
        high, low = high_low(value)
        out[:, at : at + 2 * cols] = high
        out[:, at + 6 * cols : at + 8 * cols] = low
        at += 2 * cols


def found_kernel(wide, received, known, out):
    rows = received.shape[1]
    cols = known.shape[0] // 2
    total = jnp.sum(received[...].astype(FLOAT), axis=0)
    products = joined(total[:, wide:])
    lacks = products[:, 2 * cols : 3 * cols] * SMALL
    lacks = jnp.concatenate([lacks, jnp.zeros_like(lacks)]).astype(HALF)
    shift = jnp.dot(lacks, known[:cols, :wide], preferred_element_type=FLOAT)[:rows]
    high, low = high_low(products)
    total = jnp.concatenate([(total[:, :wide] - shift).astype(HALF), high, low], axis=1)
    out[...] = jnp.broadcast_to(total, out.shape)


def side_by_side(first, second):
    cols = first.shape[1] // 2
    left = lax.broadcasted_iota(jnp.int32, first.shape, 1) < cols
    return jnp.where(left, first, pltpu.roll(second, cols, 1))


def image_kernel(blocks, found, known, hidden, ahead, out):
    tokens, features = hidden.shape
    cols = found.shape[0]
    span = features // blocks
    wide = padded(tokens + LAG)
    image, cross = lag_image(jnp.concatenate([found[:, :wide], known[cols:, :wide]]), hidden, ahead)
    high = cross.astype(HALF).astype(FLOAT)
    low = cross - high
    pieces = [side_by_side(high, low), side_by_side(pltpu.roll(high, cols, 1), pltpu.roll(low, cols, 1))]
    groups = 2 * cols // 8
    for g in range(groups):
        for b in range(blocks):
            out[g * blocks + b, :, :span] = image[8 * g : 8 * g + 8, b * span : (b + 1) * span].astype(HALF)
    for k in range(out.shape[0]):
        if k < 2 * groups:
            g = k % groups
            out[k, :, span:] = pieces[k // groups][8 * g : 8 * g + 8].astype(HALF)
        else:
            out[k, :, span:] = jnp.zeros((8, 2 * cols), HALF)


def total_kernel(factor, cols, received, out):
    span = received.shape[2] - 2 * cols
    total = jnp.sum(received[...].astype(FLOAT), axis=0) * factor
    cross = total[:, span:]
    cross = cross + pltpu.roll(cross, cols, 1)
    high = cross.astype(HALF).astype(FLOAT)
    left = lax.broadcasted_iota(jnp.int32, cross.shape, 1) < cols
    cross = jnp.where(left, high, cross - high)
    total = jnp.concatenate([total[:, :span], cross], axis=1).astype(HALF)
    out[...] = jnp.broadcast_to(total, out.shape)


def inner_products(wide, first_total, found, known, search):
    cols = found.shape[0]
    products = joined(found[:, wide:])
    r_x, r_p, lacks, image_x_p, r_r = (products[:, i * cols : (i + 1) * cols] for i in range(5))
    products = joined(known[:, wide:])
    x_x, p_x, p_p = products[:cols, :cols], products[cols:, :cols], products[cols:, cols:]
    rayleigh_t = first_total[:, first_total.shape[1] - cols :] + lacks
    lacks = lacks * SMALL
    lacks_xx = times(lacks, x_x)
    r_r = r_r - exact(lacks, r_x) - exact(r_x, lacks) + exact(lacks_xx, lacks)
    r_x = r_x - lacks_xx
    r_p = r_p - exact(lacks, p_x)
    square = (cols, cols)
    eye = lax.broadcasted_iota(jnp.int32, square, 0) == lax.broadcasted_iota(jnp.int32, square, 1)
    lengths = jnp.where(eye, r_r, 0.0)

    def scaling(lengths):
        return lax.rsqrt(lengths * (1.0 / SMALL**2) + 1e-06) * (1.0 / SMALL)

    scale = scaling(jnp.sum(lengths, axis=1, keepdims=True))
    across = scaling(jnp.sum(lengths, axis=0, keepdims=True))
    u_image_x = (r_r * (1.0 / SMALL) + exact(r_x, rayleigh_t)) * scale
    u_x, u_p = r_x * scale, r_p * scale
    turned = exact(eye.astype(FLOAT), jnp.concatenate([rayleigh_t, u_image_x, image_x_p, u_x, p_x, u_p]))
    turned = [turned[:, i * cols : (i + 1) * cols] for i in range(6)]
    rows = [[x_x, turned[3], turned[4]], [u_x, r_r * scale * across, u_p], [p_x, turned[5], p_p]]
    for i, row in enumerate(rows):
        search[i * cols : (i + 1) * cols] = jnp.concatenate(row, axis=1)
    return scale, across, turned[:3], u_image_x, image_x_p


def last_kernel(blocks, wide, gathered, first_total, found, known, images, gram, search):
    cols = found.shape[0]
    scale, across, turned, u_image_x, image_x_p = inner_products(wide, first_total, found, known, search)
    features = images.shape[1]
    span = features // blocks
    groups = cols // 8
    images[:cols] = first_total[:, :features]
    for g in range(groups):
        for b in range(blocks):
            at = slice(b * span, (b + 1) * span)
            rows = slice(cols + 8 * g, cols + 8 * g + 8)
            images[rows, at] = gathered[g * blocks + b, :, :span].astype(FLOAT) * scale[8 * g : 8 * g + 8]
            rows = slice(2 * cols + 8 * g, 2 * cols + 8 * g + 8)
            images[rows, at] = gathered[(groups + g) * blocks + b, :, :span].astype(FLOAT)

    def piece(first):
        value = jnp.concatenate([gathered[k, :, span:].astype(FLOAT) for k in range(first, first + groups)])
        return (value + pltpu.roll(value, cols, 1))[:, :cols]

    rr, pr, rp, pp = (piece(i * groups) for i in range(4))
    rows = [
        [turned[0], turned[1], image_x_p],
        [u_image_x, rr * scale * across, rp * scale],
        [turned[2], pr * across, pp],
    ]
    for i, row in enumerate(rows):
        gram[i * cols : (i + 1) * cols] = jnp.concatenate(row, axis=1)


def local(hidden_states, current_block, directions):
    tokens, features = hidden_states.shape
    cols = current_block.shape[1]
    feat, tok = lax.axis_size("feat"), lax.axis_size("tok")
    factor = 0.5 / math.sqrt(tokens * tok - LAG)
    wide = padded(tokens + LAG)
    blocks = tok * 8 // (2 * cols)

    down = [(i + 1, i) for i in range(tok - 1)]
    both = jnp.concatenate([current_block.T, directions.T])

    total = wide + 4 * cols
    flat = shape((2 * cols, total), HALF)
    part, edge = kernel_call(
        start_kernel, [flat, shape((2 * cols, LAG), HALF)], both, hidden_states
    )
    edge = lax.ppermute(edge, "tok", down)
    rows, edge = lax.optimization_barrier((hidden_states[:LAG], edge))
    ahead = lax.ppermute(rows, "tok", down)
    part = kernel_call(functools.partial(edge_kernel, tokens), flat, part, edge)
    blocked = shape((feat, 2 * cols // feat, total), HALF)
    part = exchange(part.reshape(blocked.shape), "feat")
    part = kernel_call(functools.partial(known_kernel, wide), blocked, part)
    part, ahead = lax.optimization_barrier((part, ahead))
    known = exchange(part, "feat").reshape(2 * cols, total)

    part = kernel_call(first_kernel, shape((cols, features + cols), FLOAT), known, hidden_states, ahead, far=1)
    part = exchange(part.reshape(tok, 1, -1), "tok")
    part = jnp.sum(part, axis=0) * factor
    part = exchange(jnp.broadcast_to(part, (tok,) + part.shape), "tok")
    first_total = part.reshape(cols, features + cols)

    total = wide + 12 * cols
    part = kernel_call(
        functools.partial(residual_kernel, feat), shape((cols, total), HALF), first_total, hidden_states, both, ahead, far=1
    )
    blocked = shape((feat, cols // feat, total), HALF)
    part = exchange(part.reshape(blocked.shape), "feat")
    part = kernel_call(functools.partial(found_kernel, wide), blocked, part, known)
    found = exchange(part, "feat").reshape(cols, total)

    blocked = shape((tok, 8, features // blocks + 2 * cols), HALF)
    part = kernel_call(functools.partial(image_kernel, blocks), blocked, found, known, hidden_states, ahead, far=1)
    part = exchange(part, "tok")
    part = kernel_call(functools.partial(total_kernel, factor, cols), blocked, part)
    gathered = exchange(part, "tok")
    gram = shape((3 * cols, 3 * cols), FLOAT)
    images, gram_image, gram_search = kernel_call(
        functools.partial(last_kernel, blocks, wide),
        [shape((3 * cols, features), FLOAT), gram, gram],
        gathered,
        first_total,
        found,
        known,
    )
    return (images.T, gram_image, gram_search)


def solution(mesh):
    return jax.shard_map(
        local,
        mesh=mesh,
        in_specs=(P("tok", "feat"), P("feat", None), P("feat", None)),
        out_specs=(P("feat", None), P(), P()),
        check_vma=False,
    )
```

```python
import functools
import math

import jax
import jax.numpy as jnp
from jax import lax
from jax.experimental import pallas as pl
from jax.experimental.pallas import tpu as pltpu
from jax.sharding import PartitionSpec as P

LAG = 256
SMALL = 2.0**-20
LANES = 128
HIGHEST = lax.Precision.HIGHEST
HALF = jnp.bfloat16
FLOAT = jnp.float32


def padded(size):
    return -(-size // LANES) * LANES


def exchange(value, axis):
    return lax.all_to_all(value, axis, 0, 0, tiled=True)


def kernel_call(body, outputs, *operands):
    many = isinstance(outputs, list)
    spec = pl.BlockSpec(memory_space=pltpu.VMEM)
    return pl.pallas_call(
        body,
        out_shape=outputs,
        in_specs=[spec] * len(operands),
        out_specs=[spec] * len(outputs) if many else spec,
        compiler_params=pltpu.CompilerParams(vmem_limit_bytes=16 * 2**20),
    )(*operands)


def shape(dims, dtype):
    return jax.ShapeDtypeStruct(dims, dtype)


def rows_dot(a, b, precision=None):
    return lax.dot_general(a, b, (((1,), (1,)), ((), ())), preferred_element_type=FLOAT, precision=precision)


def exact(a, b):
    return rows_dot(a, b, HIGHEST)


def times(a, b):
    return jnp.dot(a, b, precision=HIGHEST, preferred_element_type=FLOAT)


def high_low(value):
    high = value.astype(HALF)
    return high, (value - high.astype(FLOAT)).astype(HALF)


def joined(value):
    value = value.astype(FLOAT)
    middle = value.shape[1] // 2
    return value[:, :middle] + value[:, middle:]


def project_own(vectors, hidden, out):
    whole = hidden.shape[0] // LANES * LANES
    out[:, :whole] = rows_dot(vectors, hidden[:whole]).astype(HALF)


def project_edge(vectors, tail, ahead):
    rows, rest = vectors.shape[0], tail.shape[0]
    value = rows_dot(vectors, jnp.concatenate([tail, ahead[...]])).astype(HALF)
    spare = padded(rest + LAG) - rest - LAG
    if spare:
        value = jnp.concatenate([value, jnp.zeros((rows, spare), HALF)], axis=1)
    return value


def start_kernel(both, hidden, out, first):
    both = both[...]
    rounded = both.astype(HALF)
    whole = hidden.shape[0] // LANES * LANES
    wide = out.shape[1] - 2 * both.shape[0]
    products = exact(both, both)
    edge = rows_dot(rounded, hidden[:LAG]).astype(HALF)
    first[...] = edge
    out[:, :LAG] = edge
    out[:, LAG:whole] = rows_dot(rounded, hidden[LAG:whole]).astype(HALF)
    rest = hidden.shape[0] - whole
    if rest:
        tail = rows_dot(rounded, jnp.concatenate([hidden[whole:], hidden[: LANES - rest]])).astype(HALF)
        out[:, whole : whole + LANES] = tail
    high, low = high_low(products)
    out[:, wide : wide + high.shape[1]] = high
    out[:, wide + high.shape[1] :] = low


def edge_kernel(tokens, start, ahead, out):
    rows, whole = start.shape[0], tokens // LANES * LANES
    wide = padded(tokens + LAG)
    out[:, :whole] = start[:, :whole]
    out[:, wide:] = start[:, wide:]
    pieces = [start[:, whole : whole + LANES][:, : tokens - whole]] if tokens > whole else []
    pieces.append(ahead[...])
    if wide > tokens + LAG:
        pieces.append(jnp.zeros((rows, wide - tokens - LAG), HALF))
    out[:, whole:wide] = jnp.concatenate(pieces, axis=1)


def known_kernel(wide, received, out):
    total = jnp.sum(received[...].astype(FLOAT), axis=0)
    high, low = high_low(joined(total[:, wide:]))
    total = jnp.concatenate([total[:, :wide].astype(HALF), high, low], axis=1)
    out[...] = jnp.broadcast_to(total, out.shape)


def lag_image(projected, hidden, ahead):
    tokens = hidden.shape[0]
    cut = tokens // LANES * LANES - LAG
    here, later = projected[:, :tokens], projected[:, LAG : LAG + tokens]
    image = jnp.dot(later, hidden[...], preferred_element_type=FLOAT)
    image += jnp.dot(here[:, :cut], hidden[LAG : LAG + cut], preferred_element_type=FLOAT)
    cross = rows_dot(later, here) + rows_dot(here, later)
    edge = jnp.concatenate([hidden[cut + LAG :], ahead[...]])
    image += jnp.dot(here[:, cut:], edge, preferred_element_type=FLOAT)
    return image, cross


def first_kernel(known, hidden, ahead, out):
    features = hidden.shape[1]
    image, cross = lag_image(known[: out.shape[0]], hidden, ahead)
    out[:, :features] = image
    out[:, features:] = cross


def spread_kernel(factor, received, out):
    total = jnp.sum(received[...], axis=0, keepdims=True) * factor
    out[...] = jnp.broadcast_to(total, out.shape)


def residual_kernel(feat, total, hidden, both, ahead, out):
    tokens, features = hidden.shape
    cols = total.shape[0]
    whole, at = tokens // LANES * LANES, padded(tokens + LAG)
    image = total[:, :features]
    residual = (image - times(total[:, features:], both[:cols])) * SMALL
    rounded = residual.astype(HALF)
    project_own(rounded, hidden, out)
    products = exact(jnp.concatenate([residual, image]), both[...])
    own = exact(jnp.concatenate([residual, residual]), residual)[:cols]
    own = jnp.concatenate([own, jnp.zeros_like(own)], axis=1)
    out[:, whole:at] = project_edge(rounded, hidden[whole:], ahead)
    share = total[:, features:] * (1.0 / feat)
    lacks = products[cols:] - jnp.concatenate([share, jnp.zeros_like(share)], axis=1)
    for value in (products[:cols], lacks, own):
        high, low = high_low(value)
        out[:, at : at + 2 * cols] = high
        out[:, at + 6 * cols : at + 8 * cols] = low
        at += 2 * cols


def found_kernel(wide, received, known, out):
    rows = received.shape[1]
    cols = known.shape[0] // 2
    total = jnp.sum(received[...].astype(FLOAT), axis=0)
    products = joined(total[:, wide:])
    lacks = products[:, 2 * cols : 3 * cols] * SMALL
    lacks = jnp.concatenate([lacks, jnp.zeros_like(lacks)]).astype(HALF)
    shift = jnp.dot(lacks, known[:cols, :wide], preferred_element_type=FLOAT)[:rows]
    high, low = high_low(products)
    total = jnp.concatenate([(total[:, :wide] - shift).astype(HALF), high, low], axis=1)
    out[...] = jnp.broadcast_to(total, out.shape)


def side_by_side(first, second):
    cols = first.shape[1] // 2
    left = lax.broadcasted_iota(jnp.int32, first.shape, 1) < cols
    return jnp.where(left, first, pltpu.roll(second, cols, 1))


def image_kernel(blocks, found, known, hidden, ahead, out):
    tokens, features = hidden.shape
    cols = found.shape[0]
    span = features // blocks
    wide = padded(tokens + LAG)
    image, cross = lag_image(jnp.concatenate([found[:, :wide], known[cols:, :wide]]), hidden, ahead)
    high = cross.astype(HALF).astype(FLOAT)
    low = cross - high
    pieces = [side_by_side(high, low), side_by_side(pltpu.roll(high, cols, 1), pltpu.roll(low, cols, 1))]
    groups = 2 * cols // 8
    for g in range(groups):
        for b in range(blocks):
            out[g * blocks + b, :, :span] = image[8 * g : 8 * g + 8, b * span : (b + 1) * span].astype(HALF)
    for k in range(out.shape[0]):
        if k < 2 * groups:
            g = k % groups
            out[k, :, span:] = pieces[k // groups][8 * g : 8 * g + 8].astype(HALF)
        else:
            out[k, :, span:] = jnp.zeros((8, 2 * cols), HALF)


def total_kernel(factor, cols, received, out):
    span = received.shape[2] - 2 * cols
    total = jnp.sum(received[...].astype(FLOAT), axis=0) * factor
    cross = total[:, span:]
    cross = cross + pltpu.roll(cross, cols, 1)
    high = cross.astype(HALF).astype(FLOAT)
    left = lax.broadcasted_iota(jnp.int32, cross.shape, 1) < cols
    cross = jnp.where(left, high, cross - high)
    total = jnp.concatenate([total[:, :span], cross], axis=1).astype(HALF)
    out[...] = jnp.broadcast_to(total, out.shape)


def inner_products(wide, first_total, found, known, search):
    cols = found.shape[0]
    products = joined(found[:, wide:])
    r_x, r_p, lacks, image_x_p, r_r = (products[:, i * cols : (i + 1) * cols] for i in range(5))
    products = joined(known[:, wide:])
    x_x, p_x, p_p = products[:cols, :cols], products[cols:, :cols], products[cols:, cols:]
    rayleigh_t = first_total[:, first_total.shape[1] - cols :] + lacks
    lacks = lacks * SMALL
    lacks_xx = times(lacks, x_x)
    r_r = r_r - exact(lacks, r_x) - exact(r_x, lacks) + exact(lacks_xx, lacks)
    r_x = r_x - lacks_xx
    r_p = r_p - exact(lacks, p_x)
    square = (cols, cols)
    eye = lax.broadcasted_iota(jnp.int32, square, 0) == lax.broadcasted_iota(jnp.int32, square, 1)
    lengths = jnp.where(eye, r_r, 0.0)

    def scaling(lengths):
        return lax.rsqrt(lengths * (1.0 / SMALL**2) + 1e-06) * (1.0 / SMALL)

    scale = scaling(jnp.sum(lengths, axis=1, keepdims=True))
    across = scaling(jnp.sum(lengths, axis=0, keepdims=True))
    u_image_x = (r_r * (1.0 / SMALL) + exact(r_x, rayleigh_t)) * scale
    u_x, u_p = r_x * scale, r_p * scale
    turned = exact(eye.astype(FLOAT), jnp.concatenate([rayleigh_t, u_image_x, image_x_p, u_x, p_x, u_p]))
    turned = [turned[:, i * cols : (i + 1) * cols] for i in range(6)]
    rows = [[x_x, turned[3], turned[4]], [u_x, r_r * scale * across, u_p], [p_x, turned[5], p_p]]
    for i, row in enumerate(rows):
        search[i * cols : (i + 1) * cols] = jnp.concatenate(row, axis=1)
    return scale, across, turned[:3], u_image_x, image_x_p


def last_kernel(blocks, wide, gathered, first_total, found, known, images, gram, search):
    cols = found.shape[0]
    scale, across, turned, u_image_x, image_x_p = inner_products(wide, first_total, found, known, search)
    features = images.shape[1]
    span = features // blocks
    groups = cols // 8
    images[:cols] = first_total[:, :features]
    for g in range(groups):
        for b in range(blocks):
            at = slice(b * span, (b + 1) * span)
            rows = slice(cols + 8 * g, cols + 8 * g + 8)
            images[rows, at] = gathered[g * blocks + b, :, :span].astype(FLOAT) * scale[8 * g : 8 * g + 8]
            rows = slice(2 * cols + 8 * g, 2 * cols + 8 * g + 8)
            images[rows, at] = gathered[(groups + g) * blocks + b, :, :span].astype(FLOAT)

    def piece(first):
        value = jnp.concatenate([gathered[k, :, span:].astype(FLOAT) for k in range(first, first + groups)])
        return (value + pltpu.roll(value, cols, 1))[:, :cols]

    rr, pr, rp, pp = (piece(i * groups) for i in range(4))
    rows = [
        [turned[0], turned[1], image_x_p],
        [u_image_x, rr * scale * across, rp * scale],
        [turned[2], pr * across, pp],
    ]
    for i, row in enumerate(rows):
        gram[i * cols : (i + 1) * cols] = jnp.concatenate(row, axis=1)


def local(hidden_states, current_block, directions):
    tokens, features = hidden_states.shape
    cols = current_block.shape[1]
    feat, tok = lax.axis_size("feat"), lax.axis_size("tok")
    factor = 0.5 / math.sqrt(tokens * tok - LAG)
    wide = padded(tokens + LAG)
    blocks = tok * 8 // (2 * cols)

    down = [(i + 1, i) for i in range(tok - 1)]
    both = jnp.concatenate([current_block.T, directions.T])

    total = wide + 4 * cols
    flat = shape((2 * cols, total), HALF)
    part, edge = kernel_call(
        start_kernel, [flat, shape((2 * cols, LAG), HALF)], both, hidden_states
    )
    edge = lax.ppermute(edge, "tok", down)
    rows, edge = lax.optimization_barrier((hidden_states[:LAG], edge))
    ahead = lax.ppermute(rows, "tok", down)
    part = kernel_call(functools.partial(edge_kernel, tokens), flat, part, edge)
    blocked = shape((feat, 2 * cols // feat, total), HALF)
    part = exchange(part.reshape(blocked.shape), "feat")
    part = kernel_call(functools.partial(known_kernel, wide), blocked, part)
    known = exchange(part, "feat").reshape(2 * cols, total)

    part = kernel_call(first_kernel, shape((cols, features + cols), FLOAT), known, hidden_states, ahead)
    flat = shape((tok, cols * (features + cols) // tok), FLOAT)
    part = exchange(part.reshape(flat.shape), "tok")
    part = kernel_call(functools.partial(spread_kernel, factor), flat, part)
    part = exchange(part, "tok")
    first_total = part.reshape(cols, features + cols)

    total = wide + 12 * cols
    part = kernel_call(
        functools.partial(residual_kernel, feat), shape((cols, total), HALF), first_total, hidden_states, both, ahead
    )
    blocked = shape((feat, cols // feat, total), HALF)
    part = exchange(part.reshape(blocked.shape), "feat")
    part = kernel_call(functools.partial(found_kernel, wide), blocked, part, known)
    found = exchange(part, "feat").reshape(cols, total)

    blocked = shape((tok, 8, features // blocks + 2 * cols), HALF)
    part = kernel_call(functools.partial(image_kernel, blocks), blocked, found, known, hidden_states, ahead)
    part = exchange(part, "tok")
    part = kernel_call(functools.partial(total_kernel, factor, cols), blocked, part)
    gathered = exchange(part, "tok")
    gram = shape((3 * cols, 3 * cols), FLOAT)
    images, gram_image, gram_search = kernel_call(
        functools.partial(last_kernel, blocks, wide),
        [shape((3 * cols, features), FLOAT), gram, gram],
        gathered,
        first_total,
        found,
        known,
    )
    return (images.T, gram_image, gram_search)


def solution(mesh):
    return jax.shard_map(
        local,
        mesh=mesh,
        in_specs=(P("tok", "feat"), P("feat", None), P("feat", None)),
        out_specs=(P("feat", None), P(), P()),
        check_vma=False,
    )
```

```python
import functools
import math

import jax
import jax.numpy as jnp
from jax import lax
from jax.experimental import pallas as pl
from jax.experimental.pallas import tpu as pltpu
from jax.sharding import PartitionSpec as P

LAG = 256
SMALL = 2.0**-20
LANES = 128
HIGHEST = lax.Precision.HIGHEST
HALF = jnp.bfloat16
FLOAT = jnp.float32


def padded(size):
    return -(-size // LANES) * LANES


def exchange(value, axis):
    return lax.all_to_all(value, axis, 0, 0, tiled=True)


def kernel_call(body, outputs, *operands):
    many = isinstance(outputs, list)
    spec = pl.BlockSpec(memory_space=pltpu.VMEM)
    return pl.pallas_call(
        body,
        out_shape=outputs,
        in_specs=[spec] * len(operands),
        out_specs=[spec] * len(outputs) if many else spec,
        compiler_params=pltpu.CompilerParams(vmem_limit_bytes=16 * 2**20),
    )(*operands)


def shape(dims, dtype):
    return jax.ShapeDtypeStruct(dims, dtype)


def rows_dot(a, b, precision=None):
    return lax.dot_general(a, b, (((1,), (1,)), ((), ())), preferred_element_type=FLOAT, precision=precision)


def exact(a, b):
    return rows_dot(a, b, HIGHEST)


def times(a, b):
    return jnp.dot(a, b, precision=HIGHEST, preferred_element_type=FLOAT)


def high_low(value):
    high = value.astype(HALF)
    return high, (value - high.astype(FLOAT)).astype(HALF)


def joined(value):
    value = value.astype(FLOAT)
    middle = value.shape[1] // 2
    return value[:, :middle] + value[:, middle:]


def project_own(vectors, hidden, out):
    whole = hidden.shape[0] // LANES * LANES
    out[:, :whole] = rows_dot(vectors, hidden[:whole]).astype(HALF)


def project_edge(vectors, tail, ahead):
    rows, rest = vectors.shape[0], tail.shape[0]
    value = rows_dot(vectors, jnp.concatenate([tail, ahead[...]])).astype(HALF)
    spare = padded(rest + LAG) - rest - LAG
    if spare:
        value = jnp.concatenate([value, jnp.zeros((rows, spare), HALF)], axis=1)
    return value


def start_kernel(both, hidden, out):
    rows = both.shape[0]
    wide = out.shape[1] - 2 * rows
    project_own(both[...].astype(HALF), hidden, out)
    high, low = high_low(exact(both[...], both[...]))
    out[:, wide : wide + rows] = high
    out[:, wide + rows :] = low


def edge_kernel(whole, both, tail, ahead, start, out):
    wide = out.shape[1] - 2 * both.shape[0]
    out[:, :whole] = start[:, :whole]
    out[:, wide:] = start[:, wide:]
    out[:, whole:wide] = project_edge(both[...].astype(HALF), tail[...], ahead)


def known_kernel(wide, received, out):
    total = jnp.sum(received[...].astype(FLOAT), axis=0)
    high, low = high_low(joined(total[:, wide:]))
    total = jnp.concatenate([total[:, :wide].astype(HALF), high, low], axis=1)
    out[...] = jnp.broadcast_to(total, out.shape)


def lag_image(projected, hidden, ahead):
    tokens = hidden.shape[0]
    cut = tokens // LANES * LANES - LAG
    here, later = projected[:, :tokens], projected[:, LAG : LAG + tokens]
    edge = jnp.concatenate([hidden[cut + LAG :], ahead[...]])
    image = jnp.dot(later, hidden[...], preferred_element_type=FLOAT)
    image += jnp.dot(here[:, :cut], hidden[LAG : LAG + cut], preferred_element_type=FLOAT)
    image += jnp.dot(here[:, cut:], edge, preferred_element_type=FLOAT)
    return image, rows_dot(later, here) + rows_dot(here, later)


def first_kernel(known, hidden, ahead, out):
    features = hidden.shape[1]
    image, cross = lag_image(known[: out.shape[0]], hidden, ahead)
    out[:, :features] = image
    out[:, features:] = cross


def spread_kernel(factor, received, out):
    total = jnp.sum(received[...], axis=0, keepdims=True) * factor
    out[...] = jnp.broadcast_to(total, out.shape)


def residual_kernel(feat, total, both, hidden, ahead, out):
    tokens, features = hidden.shape
    cols = total.shape[0]
    whole, at = tokens // LANES * LANES, padded(tokens + LAG)
    image = total[:, :features]
    residual = (image - times(total[:, features:], both[:cols])) * SMALL
    rounded = residual.astype(HALF)
    project_own(rounded, hidden, out)
    out[:, whole:at] = project_edge(rounded, hidden[whole:], ahead)
    products = exact(jnp.concatenate([residual, image]), both[...])
    share = total[:, features:] * (1.0 / feat)
    lacks = products[cols:] - jnp.concatenate([share, jnp.zeros_like(share)], axis=1)
    own = exact(jnp.concatenate([residual, residual]), residual)[:cols]
    own = jnp.concatenate([own, jnp.zeros_like(own)], axis=1)
    for value in (products[:cols], lacks, own):
        high, low = high_low(value)
        out[:, at : at + 2 * cols] = high
        out[:, at + 6 * cols : at + 8 * cols] = low
        at += 2 * cols


def found_kernel(wide, received, known, out):
    rows = received.shape[1]
    cols = known.shape[0] // 2
    total = jnp.sum(received[...].astype(FLOAT), axis=0)
    products = joined(total[:, wide:])
    lacks = products[:, 2 * cols : 3 * cols] * SMALL
    lacks = jnp.concatenate([lacks, jnp.zeros_like(lacks)]).astype(HALF)
    shift = jnp.dot(lacks, known[:cols, :wide], preferred_element_type=FLOAT)[:rows]
    high, low = high_low(products)
    total = jnp.concatenate([(total[:, :wide] - shift).astype(HALF), high, low], axis=1)
    out[...] = jnp.broadcast_to(total, out.shape)


def side_by_side(first, second):
    cols = first.shape[1] // 2
    left = lax.broadcasted_iota(jnp.int32, first.shape, 1) < cols
    return jnp.where(left, first, pltpu.roll(second, cols, 1))


def image_kernel(blocks, found, known, hidden, ahead, out):
    tokens, features = hidden.shape
    cols = found.shape[0]
    span = features // blocks
    wide = padded(tokens + LAG)
    image, cross = lag_image(jnp.concatenate([found[:, :wide], known[cols:, :wide]]), hidden, ahead)
    high = cross.astype(HALF).astype(FLOAT)
    low = cross - high
    pieces = [side_by_side(high, low), side_by_side(pltpu.roll(high, cols, 1), pltpu.roll(low, cols, 1))]
    groups = 2 * cols // 8
    for g in range(groups):
        for b in range(blocks):
            out[g * blocks + b, :, :span] = image[8 * g : 8 * g + 8, b * span : (b + 1) * span].astype(HALF)
    for k in range(out.shape[0]):
        if k < 2 * groups:
            g = k % groups
            out[k, :, span:] = pieces[k // groups][8 * g : 8 * g + 8].astype(HALF)
        else:
            out[k, :, span:] = jnp.zeros((8, 2 * cols), HALF)


def total_kernel(factor, cols, received, out):
    span = received.shape[2] - 2 * cols
    total = jnp.sum(received[...].astype(FLOAT), axis=0) * factor
    cross = total[:, span:]
    cross = cross + pltpu.roll(cross, cols, 1)
    high = cross.astype(HALF).astype(FLOAT)
    left = lax.broadcasted_iota(jnp.int32, cross.shape, 1) < cols
    cross = jnp.where(left, high, cross - high)
    total = jnp.concatenate([total[:, :span], cross], axis=1).astype(HALF)
    out[...] = jnp.broadcast_to(total, out.shape)


def inner_products(wide, first_total, found, known, search):
    cols = found.shape[0]
    products = joined(found[:, wide:])
    r_x, r_p, lacks, image_x_p, r_r = (products[:, i * cols : (i + 1) * cols] for i in range(5))
    products = joined(known[:, wide:])
    x_x, p_x, p_p = products[:cols, :cols], products[cols:, :cols], products[cols:, cols:]
    rayleigh_t = first_total[:, first_total.shape[1] - cols :] + lacks
    lacks = lacks * SMALL
    lacks_xx = times(lacks, x_x)
    r_r = r_r - exact(lacks, r_x) - exact(r_x, lacks) + exact(lacks_xx, lacks)
    r_x = r_x - lacks_xx
    r_p = r_p - exact(lacks, p_x)
    square = (cols, cols)
    eye = lax.broadcasted_iota(jnp.int32, square, 0) == lax.broadcasted_iota(jnp.int32, square, 1)
    lengths = jnp.where(eye, r_r, 0.0)

    def scaling(lengths):
        return lax.rsqrt(lengths * (1.0 / SMALL**2) + 1e-06) * (1.0 / SMALL)

    scale = scaling(jnp.sum(lengths, axis=1, keepdims=True))
    across = scaling(jnp.sum(lengths, axis=0, keepdims=True))
    u_image_x = (r_r * (1.0 / SMALL) + exact(r_x, rayleigh_t)) * scale
    u_x, u_p = r_x * scale, r_p * scale
    turned = exact(eye.astype(FLOAT), jnp.concatenate([rayleigh_t, u_image_x, image_x_p, u_x, p_x, u_p]))
    turned = [turned[:, i * cols : (i + 1) * cols] for i in range(6)]
    rows = [[x_x, turned[3], turned[4]], [u_x, r_r * scale * across, u_p], [p_x, turned[5], p_p]]
    for i, row in enumerate(rows):
        search[i * cols : (i + 1) * cols] = jnp.concatenate(row, axis=1)
    return scale, across, turned[:3], u_image_x, image_x_p


def last_kernel(blocks, wide, gathered, first_total, found, known, images, gram, search):
    cols = found.shape[0]
    scale, across, turned, u_image_x, image_x_p = inner_products(wide, first_total, found, known, search)
    features = images.shape[1]
    span = features // blocks
    groups = cols // 8
    images[:cols] = first_total[:, :features]
    for g in range(groups):
        for b in range(blocks):
            at = slice(b * span, (b + 1) * span)
            rows = slice(cols + 8 * g, cols + 8 * g + 8)
            images[rows, at] = gathered[g * blocks + b, :, :span].astype(FLOAT) * scale[8 * g : 8 * g + 8]
            rows = slice(2 * cols + 8 * g, 2 * cols + 8 * g + 8)
            images[rows, at] = gathered[(groups + g) * blocks + b, :, :span].astype(FLOAT)

    def piece(first):
        value = jnp.concatenate([gathered[k, :, span:].astype(FLOAT) for k in range(first, first + groups)])
        return (value + pltpu.roll(value, cols, 1))[:, :cols]

    rr, pr, rp, pp = (piece(i * groups) for i in range(4))
    rows = [
        [turned[0], turned[1], image_x_p],
        [u_image_x, rr * scale * across, rp * scale],
        [turned[2], pr * across, pp],
    ]
    for i, row in enumerate(rows):
        gram[i * cols : (i + 1) * cols] = jnp.concatenate(row, axis=1)


def local(hidden_states, current_block, directions):
    tokens, features = hidden_states.shape
    cols = current_block.shape[1]
    feat, tok = lax.axis_size("feat"), lax.axis_size("tok")
    factor = 0.5 / math.sqrt(tokens * tok - LAG)
    whole, wide = tokens // LANES * LANES, padded(tokens + LAG)
    blocks = tok * 8 // (2 * cols)

    ahead = lax.ppermute(hidden_states[:LAG], "tok", [(i + 1, i) for i in range(tok - 1)])
    both = jnp.concatenate([current_block.T, directions.T])

    total = wide + 4 * cols
    flat = shape((2 * cols, total), HALF)
    part = kernel_call(start_kernel, flat, both, hidden_states)
    part = kernel_call(functools.partial(edge_kernel, whole), flat, both, hidden_states[whole:], ahead, part)
    blocked = shape((feat, 2 * cols // feat, total), HALF)
    part = exchange(part.reshape(blocked.shape), "feat")
    part = kernel_call(functools.partial(known_kernel, wide), blocked, part)
    known = exchange(part, "feat").reshape(2 * cols, total)

    part = kernel_call(first_kernel, shape((cols, features + cols), FLOAT), known, hidden_states, ahead)
    flat = shape((tok, cols * (features + cols) // tok), FLOAT)
    part = exchange(part.reshape(flat.shape), "tok")
    part = kernel_call(functools.partial(spread_kernel, factor), flat, part)
    part = exchange(part, "tok")
    first_total = part.reshape(cols, features + cols)

    total = wide + 12 * cols
    part = kernel_call(
        functools.partial(residual_kernel, feat), shape((cols, total), HALF), first_total, both, hidden_states, ahead
    )
    blocked = shape((feat, cols // feat, total), HALF)
    part = exchange(part.reshape(blocked.shape), "feat")
    part = kernel_call(functools.partial(found_kernel, wide), blocked, part, known)
    found = exchange(part, "feat").reshape(cols, total)

    blocked = shape((tok, 8, features // blocks + 2 * cols), HALF)
    part = kernel_call(functools.partial(image_kernel, blocks), blocked, found, known, hidden_states, ahead)
    part = exchange(part, "tok")
    part = kernel_call(functools.partial(total_kernel, factor, cols), blocked, part)
    gathered = exchange(part, "tok")
    gram = shape((3 * cols, 3 * cols), FLOAT)
    images, gram_image, gram_search = kernel_call(
        functools.partial(last_kernel, blocks, wide),
        [shape((3 * cols, features), FLOAT), gram, gram],
        gathered,
        first_total,
        found,
        known,
    )
    return (images.T, gram_image, gram_search)


def solution(mesh):
    return jax.shard_map(
        local,
        mesh=mesh,
        in_specs=(P("tok", "feat"), P("feat", None), P("feat", None)),
        out_specs=(P("feat", None), P(), P()),
        check_vma=False,
    )
```

```python
import functools
import math

import jax
import jax.numpy as jnp
from jax import lax
from jax.experimental import pallas as pl
from jax.experimental.pallas import tpu as pltpu
from jax.sharding import PartitionSpec as P

LAG = 256
SMALL = 2.0**-20
LANES = 128
HIGHEST = lax.Precision.HIGHEST
HALF = jnp.bfloat16
FLOAT = jnp.float32


def padded(size):
    return -(-size // LANES) * LANES


def exchange(value, axis):
    return lax.all_to_all(value, axis, 0, 0, tiled=True)


def kernel_call(body, outputs, *operands):
    many = isinstance(outputs, list)
    spec = pl.BlockSpec(memory_space=pltpu.VMEM)
    return pl.pallas_call(
        body,
        out_shape=outputs,
        in_specs=[spec] * len(operands),
        out_specs=[spec] * len(outputs) if many else spec,
        compiler_params=pltpu.CompilerParams(vmem_limit_bytes=16 * 2**20),
    )(*operands)


def shape(dims, dtype):
    return jax.ShapeDtypeStruct(dims, dtype)


def rows_dot(a, b, precision=None):
    return lax.dot_general(a, b, (((1,), (1,)), ((), ())), preferred_element_type=FLOAT, precision=precision)


def exact(a, b):
    return rows_dot(a, b, HIGHEST)


def times(a, b):
    return jnp.dot(a, b, precision=HIGHEST, preferred_element_type=FLOAT)


def high_low(value):
    high = value.astype(HALF)
    return high, (value - high.astype(FLOAT)).astype(HALF)


def joined(value):
    value = value.astype(FLOAT)
    middle = value.shape[1] // 2
    return value[:, :middle] + value[:, middle:]


def project_own(vectors, hidden, out):
    whole = hidden.shape[0] // LANES * LANES
    out[:, :whole] = rows_dot(vectors, hidden[:whole]).astype(HALF)


def project_edge(vectors, tail, ahead):
    rows, rest = vectors.shape[0], tail.shape[0]
    value = rows_dot(vectors, jnp.concatenate([tail, ahead[...]])).astype(HALF)
    spare = padded(rest + LAG) - rest - LAG
    if spare:
        value = jnp.concatenate([value, jnp.zeros((rows, spare), HALF)], axis=1)
    return value


def start_kernel(both, hidden, out):
    rows = both.shape[0]
    wide = out.shape[1] - 2 * rows
    project_own(both[...].astype(HALF), hidden, out)
    high, low = high_low(exact(both[...], both[...]))
    out[:, wide : wide + rows] = high
    out[:, wide + rows :] = low


def edge_kernel(whole, both, tail, ahead, start, out):
    wide = out.shape[1] - 2 * both.shape[0]
    out[:, :whole] = start[:, :whole]
    out[:, wide:] = start[:, wide:]
    out[:, whole:wide] = project_edge(both[...].astype(HALF), tail[...], ahead)


def known_kernel(wide, received, out):
    total = jnp.sum(received[...].astype(FLOAT), axis=0)
    high, low = high_low(joined(total[:, wide:]))
    total = jnp.concatenate([total[:, :wide].astype(HALF), high, low], axis=1)
    out[...] = jnp.broadcast_to(total, out.shape)


def lag_image(projected, rows, hidden, ahead):
    tokens = hidden.shape[0]
    cut = tokens // LANES * LANES - LAG
    here, later = projected[:, :tokens], projected[:, LAG : LAG + tokens]
    edge = jnp.concatenate([hidden[cut + LAG :], ahead[...]])
    image = jnp.dot(later, hidden[...], preferred_element_type=FLOAT)
    image += jnp.dot(here[:, :cut], hidden[LAG : LAG + cut], preferred_element_type=FLOAT)
    image += jnp.dot(here[:, cut:], edge, preferred_element_type=FLOAT)
    cross = rows_dot(rows[:, LAG : LAG + tokens], here) + rows_dot(rows[:, :tokens], later)
    return image, cross


def lag_cross(projected, tokens):
    here, later = projected[:, :tokens], projected[:, LAG : LAG + tokens]
    return rows_dot(later, here) + rows_dot(here, later)


def first_kernel(known, hidden, ahead, out):
    tokens, features = hidden.shape
    cols = out.shape[0]
    image, cross = lag_image(known[:cols], known[:cols], hidden, ahead)
    out[:, :features] = image
    out[:, features:] = jnp.concatenate([cross, lag_cross(known[cols:, : padded(tokens + LAG)], tokens)], axis=1)


def spread_kernel(factor, received, out):
    total = jnp.sum(received[...], axis=0, keepdims=True) * factor
    out[...] = jnp.broadcast_to(total, out.shape)


def residual_kernel(feat, total, both, hidden, ahead, out):
    tokens, features = hidden.shape
    cols = total.shape[0]
    whole, at = tokens // LANES * LANES, padded(tokens + LAG)
    image = total[:, :features]
    residual = (image - times(total[:, features : features + cols], both[:cols])) * SMALL
    rounded = residual.astype(HALF)
    project_own(rounded, hidden, out)
    out[:, whole:at] = project_edge(rounded, hidden[whole:], ahead)
    products = exact(jnp.concatenate([residual, image]), both[...])
    share = total[:, features : features + cols] * (1.0 / feat)
    lacks = products[cols:] - jnp.concatenate([share, jnp.zeros_like(share)], axis=1)
    own = exact(jnp.concatenate([residual, residual]), residual)[:cols]
    own = jnp.concatenate([own, jnp.zeros_like(own)], axis=1)
    for value in (products[:cols], lacks, own):
        high, low = high_low(value)
        out[:, at : at + 2 * cols] = high
        out[:, at + 6 * cols : at + 8 * cols] = low
        at += 2 * cols


def found_kernel(wide, received, known, out):
    rows = received.shape[1]
    cols = known.shape[0] // 2
    total = jnp.sum(received[...].astype(FLOAT), axis=0)
    products = joined(total[:, wide:])
    lacks = products[:, 2 * cols : 3 * cols] * SMALL
    lacks = jnp.concatenate([lacks, jnp.zeros_like(lacks)]).astype(HALF)
    shift = jnp.dot(lacks, known[:cols, :wide], preferred_element_type=FLOAT)[:rows]
    high, low = high_low(products)
    total = jnp.concatenate([(total[:, :wide] - shift).astype(HALF), high, low], axis=1)
    out[...] = jnp.broadcast_to(total, out.shape)


def image_kernel(found, known, hidden, ahead, out):
    tokens, features = hidden.shape
    cols = found.shape[0]
    wide = padded(tokens + LAG)
    rows = found[:, :wide]
    image, cross = lag_image(jnp.concatenate([rows, known[cols:, :wide]]), rows, hidden, ahead)
    image = image.astype(HALF)
    high = cross.astype(HALF).astype(FLOAT)
    low = cross - high
    for d in range(out.shape[0]):
        out[d, :, :features] = image[2 * d : 2 * d + 2]
        out[d, :, features:] = jnp.concatenate([high[d : d + 1], low[d : d + 1]]).astype(HALF)


def total_kernel(factor, features, received, out):
    total = jnp.sum(received[...].astype(FLOAT), axis=0) * factor
    cross = total[:1, features:] + total[1:, features:]
    high = cross.astype(HALF).astype(FLOAT)
    cross = jnp.concatenate([high, cross - high])
    total = jnp.concatenate([total[:, :features], cross], axis=1).astype(HALF)
    out[...] = jnp.broadcast_to(total, out.shape)


def inner_products(wide, first_total, found, known, search):
    cols = found.shape[0]
    products = joined(found[:, wide:])
    r_x, r_p, lacks, image_x_p, r_r = (products[:, i * cols : (i + 1) * cols] for i in range(5))
    products = joined(known[:, wide:])
    x_x, p_x, p_p = products[:cols, :cols], products[cols:, :cols], products[cols:, cols:]
    features = first_total.shape[1] - 2 * cols
    rayleigh_t = first_total[:, features : features + cols] + lacks
    lacks = lacks * SMALL
    lacks_xx = times(lacks, x_x)
    r_r = r_r - exact(lacks, r_x) - exact(r_x, lacks) + exact(lacks_xx, lacks)
    r_x = r_x - lacks_xx
    r_p = r_p - exact(lacks, p_x)
    square = (cols, cols)
    eye = lax.broadcasted_iota(jnp.int32, square, 0) == lax.broadcasted_iota(jnp.int32, square, 1)
    lengths = jnp.where(eye, r_r, 0.0)

    def scaling(lengths):
        return lax.rsqrt(lengths * (1.0 / SMALL**2) + 1e-06) * (1.0 / SMALL)

    scale = scaling(jnp.sum(lengths, axis=1, keepdims=True))
    across = scaling(jnp.sum(lengths, axis=0, keepdims=True))
    u_image_x = (r_r * (1.0 / SMALL) + exact(r_x, rayleigh_t)) * scale
    u_x, u_p = r_x * scale, r_p * scale
    turned = exact(eye.astype(FLOAT), jnp.concatenate([rayleigh_t, u_image_x, image_x_p, u_x, p_x, u_p]))
    turned = [turned[:, i * cols : (i + 1) * cols] for i in range(6)]
    rows = [[x_x, turned[3], turned[4]], [u_x, r_r * scale * across, u_p], [p_x, turned[5], p_p]]
    for i, row in enumerate(rows):
        search[i * cols : (i + 1) * cols] = jnp.concatenate(row, axis=1)
    return scale, across, eye.astype(FLOAT), turned[:3], u_image_x, image_x_p


def last_kernel(wide, gathered, first_total, found, known, images, gram, search):
    cols, features = found.shape[0], images.shape[1]
    scale, across, eye, turned, u_image_x, image_x_p = inner_products(wide, first_total, found, known, search)
    images[:cols] = first_total[:, :features]
    cross = []
    for d in range(gathered.shape[0]):
        rows = gathered[d, :, :features].astype(FLOAT)
        if 2 * d < cols:
            rows = rows * scale[2 * d : 2 * d + 2]
        images[cols + 2 * d : cols + 2 * d + 2] = rows
        pair = gathered[d, :, features:].astype(FLOAT)
        cross.append(pair[:1] + pair[1:])
    cross = jnp.concatenate(cross) * scale
    u_u, u_p = cross[:, :cols] * across, cross[:, cols:]
    p_p = first_total[:, features + cols :]
    rows = [
        [turned[0], turned[1], image_x_p],
        [u_image_x, u_u, u_p],
        [turned[2], exact(eye, u_p), p_p],
    ]
    for i, row in enumerate(rows):
        gram[i * cols : (i + 1) * cols] = jnp.concatenate(row, axis=1)


def local(hidden_states, current_block, directions):
    tokens, features = hidden_states.shape
    cols = current_block.shape[1]
    feat, tok = lax.axis_size("feat"), lax.axis_size("tok")
    factor = 0.5 / math.sqrt(tokens * tok - LAG)
    whole, wide = tokens // LANES * LANES, padded(tokens + LAG)

    ahead = lax.ppermute(hidden_states[:LAG], "tok", [(i + 1, i) for i in range(tok - 1)])
    both = jnp.concatenate([current_block.T, directions.T])

    total = wide + 4 * cols
    flat = shape((2 * cols, total), HALF)
    part = kernel_call(start_kernel, flat, both, hidden_states)
    part = kernel_call(functools.partial(edge_kernel, whole), flat, both, hidden_states[whole:], ahead, part)
    blocked = shape((feat, 2 * cols // feat, total), HALF)
    part = exchange(part.reshape(blocked.shape), "feat")
    part = kernel_call(functools.partial(known_kernel, wide), blocked, part)
    known = exchange(part, "feat").reshape(2 * cols, total)

    part = kernel_call(first_kernel, shape((cols, features + 2 * cols), FLOAT), known, hidden_states, ahead)
    flat = shape((tok, cols * (features + 2 * cols) // tok), FLOAT)
    part = exchange(part.reshape(flat.shape), "tok")
    part = kernel_call(functools.partial(spread_kernel, factor), flat, part)
    part = exchange(part, "tok")
    first_total = part.reshape(cols, features + 2 * cols)

    total = wide + 12 * cols
    part = kernel_call(
        functools.partial(residual_kernel, feat), shape((cols, total), HALF), first_total, both, hidden_states, ahead
    )
    blocked = shape((feat, cols // feat, total), HALF)
    part = exchange(part.reshape(blocked.shape), "feat")
    part = kernel_call(functools.partial(found_kernel, wide), blocked, part, known)
    found = exchange(part, "feat").reshape(cols, total)

    blocked = shape((tok, 2, features + 2 * cols), HALF)
    part = kernel_call(image_kernel, blocked, found, known, hidden_states, ahead)
    part = exchange(part, "tok")
    part = kernel_call(functools.partial(total_kernel, factor, features), blocked, part)
    gathered = exchange(part, "tok")
    gram = shape((3 * cols, 3 * cols), FLOAT)
    images, gram_image, gram_search = kernel_call(
        functools.partial(last_kernel, wide),
        [shape((3 * cols, features), FLOAT), gram, gram],
        gathered,
        first_total,
        found,
        known,
    )
    return (images.T, gram_image, gram_search)


def solution(mesh):
    return jax.shard_map(
        local,
        mesh=mesh,
        in_specs=(P("tok", "feat"), P("feat", None), P("feat", None)),
        out_specs=(P("feat", None), P(), P()),
        check_vma=False,
    )
```

```python
import functools
import math

import jax
import jax.numpy as jnp
from jax import lax
from jax.experimental import pallas as pl
from jax.experimental.pallas import tpu as pltpu
from jax.sharding import PartitionSpec as P

LAG = 256
SMALL = 2.0**-20
LANES = 128
HIGHEST = lax.Precision.HIGHEST
HALF = jnp.bfloat16
FLOAT = jnp.float32


def padded(size):
    return -(-size // LANES) * LANES


def exchange(value, axis):
    return lax.all_to_all(value, axis, 0, 0, tiled=True)


def kernel_call(body, outputs, *operands):
    many = isinstance(outputs, list)
    spec = pl.BlockSpec(memory_space=pltpu.VMEM)
    return pl.pallas_call(
        body,
        out_shape=outputs,
        in_specs=[spec] * len(operands),
        out_specs=[spec] * len(outputs) if many else spec,
        compiler_params=pltpu.CompilerParams(vmem_limit_bytes=16 * 2**20),
    )(*operands)


def shape(dims, dtype):
    return jax.ShapeDtypeStruct(dims, dtype)


def rows_dot(a, b, precision=None):
    return lax.dot_general(a, b, (((1,), (1,)), ((), ())), preferred_element_type=FLOAT, precision=precision)


def exact(a, b):
    return rows_dot(a, b, HIGHEST)


def times(a, b):
    return jnp.dot(a, b, precision=HIGHEST, preferred_element_type=FLOAT)


def high_low(value):
    high = value.astype(HALF)
    return high, (value - high.astype(FLOAT)).astype(HALF)


def joined(value):
    value = value.astype(FLOAT)
    middle = value.shape[1] // 2
    return value[:, :middle] + value[:, middle:]


def project_own(vectors, hidden, out):
    whole = hidden.shape[0] // LANES * LANES
    out[:, :whole] = rows_dot(vectors, hidden[:whole]).astype(HALF)


def project_edge(vectors, tail, ahead):
    rows, rest = vectors.shape[0], tail.shape[0]
    value = rows_dot(vectors, jnp.concatenate([tail, ahead[...]])).astype(HALF)
    spare = padded(rest + LAG) - rest - LAG
    if spare:
        value = jnp.concatenate([value, jnp.zeros((rows, spare), HALF)], axis=1)
    return value


def two_terms(value):
    high = value.astype(HALF).astype(FLOAT)
    left = lax.broadcasted_iota(jnp.int32, value.shape, 1) < value.shape[1] // 2
    return jnp.where(left, high, value - high).astype(HALF)


def start_kernel(both, hidden, out):
    rows = both.shape[0]
    cols, wide = rows // 2, out.shape[1] - rows
    project_own(both[...].astype(HALF), hidden, out)
    products = exact(both[...], both[...])
    turned = pltpu.roll(products, cols, 1)
    left = lax.broadcasted_iota(jnp.int32, (cols, rows), 1) < cols
    out[:cols, wide:] = two_terms(jnp.where(left, products[:cols], turned[:cols]))
    out[cols:, wide:] = two_terms(jnp.where(left, turned[cols:], products[cols:]))


def edge_kernel(whole, both, tail, ahead, start, out):
    wide = out.shape[1] - both.shape[0]
    out[:, :whole] = start[:, :whole]
    out[:, wide:] = start[:, wide:]
    out[:, whole:wide] = project_edge(both[...].astype(HALF), tail[...], ahead)


def known_kernel(wide, received, out):
    total = jnp.sum(received[...].astype(FLOAT), axis=0)
    products = total[:, wide:]
    products = two_terms(products + pltpu.roll(products, products.shape[1] // 2, 1))
    total = jnp.concatenate([total[:, :wide].astype(HALF), products], axis=1)
    out[...] = jnp.broadcast_to(total, out.shape)


def lag_image(projected, rows, hidden, ahead):
    tokens = hidden.shape[0]
    cut = tokens // LANES * LANES - LAG
    here, later = projected[:, :tokens], projected[:, LAG : LAG + tokens]
    edge = jnp.concatenate([hidden[cut + LAG :], ahead[...]])
    image = jnp.dot(later, hidden[...], preferred_element_type=FLOAT)
    image += jnp.dot(here[:, :cut], hidden[LAG : LAG + cut], preferred_element_type=FLOAT)
    image += jnp.dot(here[:, cut:], edge, preferred_element_type=FLOAT)
    cross = rows_dot(rows[:, LAG : LAG + tokens], here) + rows_dot(rows[:, :tokens], later)
    return image, cross


def lag_cross(projected, tokens):
    here, later = projected[:, :tokens], projected[:, LAG : LAG + tokens]
    return rows_dot(later, here) + rows_dot(here, later)


def first_kernel(known, hidden, ahead, out):
    tokens, features = hidden.shape
    cols = out.shape[0]
    image, cross = lag_image(known[:cols], known[:cols], hidden, ahead)
    out[:, :features] = image
    out[:, features:] = jnp.concatenate([cross, lag_cross(known[cols:, : padded(tokens + LAG)], tokens)], axis=1)


def spread_kernel(factor, received, out):
    total = jnp.sum(received[...], axis=0, keepdims=True) * factor
    out[...] = jnp.broadcast_to(total, out.shape)


def residual_kernel(feat, total, both, hidden, ahead, out):
    tokens, features = hidden.shape
    cols = total.shape[0]
    whole, at = tokens // LANES * LANES, padded(tokens + LAG)
    image = total[:, :features]
    residual = (image - times(total[:, features : features + cols], both[:cols])) * SMALL
    rounded = residual.astype(HALF)
    project_own(rounded, hidden, out)
    out[:, whole:at] = project_edge(rounded, hidden[whole:], ahead)
    products = exact(jnp.concatenate([residual, image, both[:cols]]), jnp.concatenate([both[...], residual]))
    share = total[:, features : features + cols] * (1.0 / feat)
    lacks = products[cols : 2 * cols, : 2 * cols] - jnp.concatenate([share, jnp.zeros_like(share)], axis=1)
    own = jnp.concatenate([products[:cols, 2 * cols :], products[2 * cols :, cols : 2 * cols]], axis=1)
    for value in (products[:cols, : 2 * cols], lacks, own):
        high, low = high_low(value)
        out[:, at : at + 2 * cols] = high
        out[:, at + 6 * cols : at + 8 * cols] = low
        at += 2 * cols


def found_kernel(wide, received, known, out):
    rows = received.shape[1]
    cols = known.shape[0] // 2
    total = jnp.sum(received[...].astype(FLOAT), axis=0)
    products = joined(total[:, wide:])
    lacks = products[:, 2 * cols : 3 * cols] * SMALL
    lacks = jnp.concatenate([lacks, jnp.zeros_like(lacks)]).astype(HALF)
    shift = jnp.dot(lacks, known[:cols, :wide], preferred_element_type=FLOAT)[:rows]
    high, low = high_low(products)
    total = jnp.concatenate([(total[:, :wide] - shift).astype(HALF), high, low], axis=1)
    out[...] = jnp.broadcast_to(total, out.shape)


def image_kernel(found, known, hidden, ahead, out):
    tokens, features = hidden.shape
    cols = found.shape[0]
    wide = padded(tokens + LAG)
    rows = found[:, :wide]
    image, cross = lag_image(jnp.concatenate([rows, known[cols:, :wide]]), rows, hidden, ahead)
    image = image.astype(HALF)
    high = cross.astype(HALF).astype(FLOAT)
    low = cross - high
    for d in range(out.shape[0]):
        out[d, :, :features] = image[2 * d : 2 * d + 2]
        out[d, :, features:] = jnp.concatenate([high[d : d + 1], low[d : d + 1]]).astype(HALF)


def total_kernel(factor, features, received, out):
    total = jnp.sum(received[...].astype(FLOAT), axis=0) * factor
    cross = total[:1, features:] + total[1:, features:]
    high = cross.astype(HALF).astype(FLOAT)
    cross = jnp.concatenate([high, cross - high])
    total = jnp.concatenate([total[:, :features], cross], axis=1).astype(HALF)
    out[...] = jnp.broadcast_to(total, out.shape)


def inner_products(wide, first_total, found, known, search):
    cols = found.shape[0]
    products = joined(found[:, wide:])
    r_x, r_p, lacks, image_x_p, r_r, x_p = (products[:, i * cols : (i + 1) * cols] for i in range(6))
    products = joined(known[:, wide:])
    x_x, p_p = products[:cols], products[cols:]
    features = first_total.shape[1] - 2 * cols
    rayleigh_t = first_total[:, features : features + cols] + lacks
    lacks = lacks * SMALL
    lacks_xx = times(lacks, x_x)
    r_r = r_r - exact(lacks, r_x) - exact(r_x, lacks) + exact(lacks_xx, lacks)
    r_x = r_x - lacks_xx
    r_p = r_p - times(lacks, x_p)
    square = (cols, cols)
    eye = lax.broadcasted_iota(jnp.int32, square, 0) == lax.broadcasted_iota(jnp.int32, square, 1)
    lengths = jnp.where(eye, r_r, 0.0)

    def scaling(lengths):
        return lax.rsqrt(lengths * (1.0 / SMALL**2) + 1e-06) * (1.0 / SMALL)

    scale = scaling(jnp.sum(lengths, axis=1, keepdims=True))
    across = scaling(jnp.sum(lengths, axis=0, keepdims=True))
    u_image_x = (r_r * (1.0 / SMALL) + exact(r_x, rayleigh_t)) * scale
    u_x, u_p = r_x * scale, r_p * scale
    turned = exact(eye.astype(FLOAT), jnp.concatenate([rayleigh_t, u_image_x, image_x_p, u_x, x_p, u_p]))
    turned = [turned[:, i * cols : (i + 1) * cols] for i in range(6)]
    rows = [[x_x, turned[3], x_p], [u_x, r_r * scale * across, u_p], [turned[4], turned[5], p_p]]
    for i, row in enumerate(rows):
        search[i * cols : (i + 1) * cols] = jnp.concatenate(row, axis=1)
    return scale, across, eye.astype(FLOAT), turned[:3], u_image_x, image_x_p


def last_kernel(wide, gathered, first_total, found, known, images, gram, search):
    cols, features = found.shape[0], images.shape[1]
    scale, across, eye, turned, u_image_x, image_x_p = inner_products(wide, first_total, found, known, search)
    images[:cols] = first_total[:, :features]
    cross = []
    for d in range(gathered.shape[0]):
        rows = gathered[d, :, :features].astype(FLOAT)
        if 2 * d < cols:
            rows = rows * scale[2 * d : 2 * d + 2]
        images[cols + 2 * d : cols + 2 * d + 2] = rows
        pair = gathered[d, :, features:].astype(FLOAT)
        cross.append(pair[:1] + pair[1:])
    cross = jnp.concatenate(cross) * scale
    u_u, u_p = cross[:, :cols] * across, cross[:, cols:]
    p_p = first_total[:, features + cols :]
    rows = [
        [turned[0], turned[1], image_x_p],
        [u_image_x, u_u, u_p],
        [turned[2], exact(eye, u_p), p_p],
    ]
    for i, row in enumerate(rows):
        gram[i * cols : (i + 1) * cols] = jnp.concatenate(row, axis=1)


def local(hidden_states, current_block, directions):
    tokens, features = hidden_states.shape
    cols = current_block.shape[1]
    feat, tok = lax.axis_size("feat"), lax.axis_size("tok")
    factor = 0.5 / math.sqrt(tokens * tok - LAG)
    whole, wide = tokens // LANES * LANES, padded(tokens + LAG)

    ahead = lax.ppermute(hidden_states[:LAG], "tok", [(i + 1, i) for i in range(tok - 1)])
    both = jnp.concatenate([current_block.T, directions.T])

    total = wide + 2 * cols
    flat = shape((2 * cols, total), HALF)
    part = kernel_call(start_kernel, flat, both, hidden_states)
    part = kernel_call(functools.partial(edge_kernel, whole), flat, both, hidden_states[whole:], ahead, part)
    blocked = shape((feat, 2 * cols // feat, total), HALF)
    part = exchange(part.reshape(blocked.shape), "feat")
    part = kernel_call(functools.partial(known_kernel, wide), blocked, part)
    known = exchange(part, "feat").reshape(2 * cols, total)

    part = kernel_call(first_kernel, shape((cols, features + 2 * cols), FLOAT), known, hidden_states, ahead)
    flat = shape((tok, cols * (features + 2 * cols) // tok), FLOAT)
    part = exchange(part.reshape(flat.shape), "tok")
    part = kernel_call(functools.partial(spread_kernel, factor), flat, part)
    part = exchange(part, "tok")
    first_total = part.reshape(cols, features + 2 * cols)

    total = wide + 12 * cols
    part = kernel_call(
        functools.partial(residual_kernel, feat), shape((cols, total), HALF), first_total, both, hidden_states, ahead
    )
    blocked = shape((feat, cols // feat, total), HALF)
    part = exchange(part.reshape(blocked.shape), "feat")
    part = kernel_call(functools.partial(found_kernel, wide), blocked, part, known)
    found = exchange(part, "feat").reshape(cols, total)

    blocked = shape((tok, 2, features + 2 * cols), HALF)
    part = kernel_call(image_kernel, blocked, found, known, hidden_states, ahead)
    part = exchange(part, "tok")
    part = kernel_call(functools.partial(total_kernel, factor, features), blocked, part)
    gathered = exchange(part, "tok")
    gram = shape((3 * cols, 3 * cols), FLOAT)
    images, gram_image, gram_search = kernel_call(
        functools.partial(last_kernel, wide),
        [shape((3 * cols, features), FLOAT), gram, gram],
        gathered,
        first_total,
        found,
        known,
    )
    return (images.T, gram_image, gram_search)


def solution(mesh):
    return jax.shard_map(
        local,
        mesh=mesh,
        in_specs=(P("tok", "feat"), P("feat", None), P("feat", None)),
        out_specs=(P("feat", None), P(), P()),
        check_vma=False,
    )
```

```python
import functools
import math

import jax
import jax.numpy as jnp
from jax import lax
from jax.experimental import pallas as pl
from jax.experimental.pallas import tpu as pltpu
from jax.sharding import PartitionSpec as P

LAG = 256
HALO = LAG // 2
SMALL = 2.0**-20
LANES = 128
HIGHEST = lax.Precision.HIGHEST
HALF = jnp.bfloat16
FLOAT = jnp.float32


def padded(size):
    return -(-size // LANES) * LANES


def exchange(value, axis):
    return lax.all_to_all(value, axis, 0, 0, tiled=True)


def kernel_call(body, outputs, *operands):
    many = isinstance(outputs, list)
    spec = pl.BlockSpec(memory_space=pltpu.VMEM)
    return pl.pallas_call(
        body,
        out_shape=outputs,
        in_specs=[spec] * len(operands),
        out_specs=[spec] * len(outputs) if many else spec,
        compiler_params=pltpu.CompilerParams(vmem_limit_bytes=16 * 2**20),
    )(*operands)


def shape(dims, dtype):
    return jax.ShapeDtypeStruct(dims, dtype)


def rows_dot(a, b, precision=None):
    return lax.dot_general(a, b, (((1,), (1,)), ((), ())), preferred_element_type=FLOAT, precision=precision)


def exact(a, b):
    return rows_dot(a, b, HIGHEST)


def times(a, b):
    return jnp.dot(a, b, precision=HIGHEST, preferred_element_type=FLOAT)


def high_low(value):
    high = value.astype(HALF)
    return high, (value - high.astype(FLOAT)).astype(HALF)


def joined(value):
    value = value.astype(FLOAT)
    middle = value.shape[1] // 2
    return value[:, :middle] + value[:, middle:]


def project_own(vectors, hidden, out):
    whole = hidden.shape[0] // LANES * LANES
    out[:, HALO : HALO + whole] = rows_dot(vectors, hidden[:whole]).astype(HALF)


def project_edges(vectors, tail, behind, ahead, out):
    rows = vectors.shape[0]
    out[:, :HALO] = rows_dot(vectors, behind[...]).astype(HALF)
    value = rows_dot(vectors, jnp.concatenate([tail, ahead[...]])).astype(HALF)
    spare = padded(value.shape[1]) - value.shape[1]
    if spare:
        value = jnp.concatenate([value, jnp.zeros((rows, spare), HALF)], axis=1)
    return value


def two_terms(value):
    high = value.astype(HALF).astype(FLOAT)
    left = lax.broadcasted_iota(jnp.int32, value.shape, 1) < value.shape[1] // 2
    return jnp.where(left, high, value - high).astype(HALF)


def start_kernel(both, hidden, out):
    rows = both.shape[0]
    cols, wide = rows // 2, out.shape[1] - rows
    project_own(both[...].astype(HALF), hidden, out)
    products = exact(both[...], both[...])
    turned = pltpu.roll(products, cols, 1)
    left = lax.broadcasted_iota(jnp.int32, (cols, rows), 1) < cols
    out[:cols, wide:] = two_terms(jnp.where(left, products[:cols], turned[:cols]))
    out[cols:, wide:] = two_terms(jnp.where(left, turned[cols:], products[cols:]))


def edge_kernel(whole, both, tail, behind, ahead, start, out):
    wide = out.shape[1] - both.shape[0]
    out[:, HALO : HALO + whole] = start[:, HALO : HALO + whole]
    out[:, wide:] = start[:, wide:]
    out[:, HALO + whole : wide] = project_edges(both[...].astype(HALF), tail[...], behind, ahead, out)


def known_kernel(wide, received, out):
    total = jnp.sum(received[...].astype(FLOAT), axis=0)
    products = total[:, wide:]
    products = two_terms(products + pltpu.roll(products, products.shape[1] // 2, 1))
    total = jnp.concatenate([total[:, :wide].astype(HALF), products], axis=1)
    out[...] = jnp.broadcast_to(total, out.shape)


def lag_image(projected, rows, hidden, behind, ahead):
    tokens = hidden.shape[0]
    whole = tokens // LANES * LANES
    cut = whole - HALO
    here, later = projected[:, :tokens], projected[:, LAG : LAG + tokens]
    edge = jnp.concatenate([hidden[whole:], ahead[...]])
    image = jnp.dot(later[:, HALO:], hidden[: tokens - HALO], preferred_element_type=FLOAT)
    image += jnp.dot(here[:, :cut], hidden[HALO:whole], preferred_element_type=FLOAT)
    image += jnp.dot(here[:, cut:], edge, preferred_element_type=FLOAT)
    image += jnp.dot(later[:, :HALO], behind[...], preferred_element_type=FLOAT)
    cross = rows_dot(rows[:, LAG : LAG + tokens], here) + rows_dot(rows[:, :tokens], later)
    return image, cross


def lag_cross(projected, tokens):
    here, later = projected[:, :tokens], projected[:, LAG : LAG + tokens]
    return rows_dot(later, here) + rows_dot(here, later)


def first_kernel(known, hidden, behind, ahead, out):
    tokens, features = hidden.shape
    cols = out.shape[0]
    image, cross = lag_image(known[:cols], known[:cols], hidden, behind, ahead)
    out[:, :features] = image
    out[:, features:] = jnp.concatenate([cross, lag_cross(known[cols:, : padded(tokens + LAG)], tokens)], axis=1)


def spread_kernel(factor, received, out):
    total = jnp.sum(received[...], axis=0, keepdims=True) * factor
    out[...] = jnp.broadcast_to(total, out.shape)


def residual_kernel(feat, total, both, hidden, behind, ahead, out):
    tokens, features = hidden.shape
    cols = total.shape[0]
    whole, at = tokens // LANES * LANES, padded(tokens + LAG)
    image = total[:, :features]
    residual = (image - times(total[:, features : features + cols], both[:cols])) * SMALL
    rounded = residual.astype(HALF)
    project_own(rounded, hidden, out)
    out[:, HALO + whole : at] = project_edges(rounded, hidden[whole:], behind, ahead, out)
    products = exact(jnp.concatenate([residual, image, both[:cols]]), jnp.concatenate([both[...], residual]))
    share = total[:, features : features + cols] * (1.0 / feat)
    lacks = products[cols : 2 * cols, : 2 * cols] - jnp.concatenate([share, jnp.zeros_like(share)], axis=1)
    own = jnp.concatenate([products[:cols, 2 * cols :], products[2 * cols :, cols : 2 * cols]], axis=1)
    for value in (products[:cols, : 2 * cols], lacks, own):
        high, low = high_low(value)
        out[:, at : at + 2 * cols] = high
        out[:, at + 6 * cols : at + 8 * cols] = low
        at += 2 * cols


def found_kernel(wide, received, known, out):
    rows = received.shape[1]
    cols = known.shape[0] // 2
    total = jnp.sum(received[...].astype(FLOAT), axis=0)
    products = joined(total[:, wide:])
    lacks = products[:, 2 * cols : 3 * cols] * SMALL
    lacks = jnp.concatenate([lacks, jnp.zeros_like(lacks)]).astype(HALF)
    shift = jnp.dot(lacks, known[:cols, :wide], preferred_element_type=FLOAT)[:rows]
    high, low = high_low(products)
    total = jnp.concatenate([(total[:, :wide] - shift).astype(HALF), high, low], axis=1)
    out[...] = jnp.broadcast_to(total, out.shape)


def image_kernel(found, known, hidden, behind, ahead, out):
    tokens, features = hidden.shape
    cols = found.shape[0]
    wide = padded(tokens + LAG)
    rows = found[:, :wide]
    image, cross = lag_image(jnp.concatenate([rows, known[cols:, :wide]]), rows, hidden, behind, ahead)
    image = image.astype(HALF)
    high = cross.astype(HALF).astype(FLOAT)
    low = cross - high
    for d in range(out.shape[0]):
        out[d, :, :features] = image[2 * d : 2 * d + 2]
        out[d, :, features:] = jnp.concatenate([high[d : d + 1], low[d : d + 1]]).astype(HALF)


def total_kernel(factor, features, received, out):
    total = jnp.sum(received[...].astype(FLOAT), axis=0) * factor
    cross = total[:1, features:] + total[1:, features:]
    high = cross.astype(HALF).astype(FLOAT)
    cross = jnp.concatenate([high, cross - high])
    total = jnp.concatenate([total[:, :features], cross], axis=1).astype(HALF)
    out[...] = jnp.broadcast_to(total, out.shape)


def inner_products(wide, first_total, found, known, search):
    cols = found.shape[0]
    products = joined(found[:, wide:])
    r_x, r_p, lacks, image_x_p, r_r, x_p = (products[:, i * cols : (i + 1) * cols] for i in range(6))
    products = joined(known[:, wide:])
    x_x, p_p = products[:cols], products[cols:]
    features = first_total.shape[1] - 2 * cols
    rayleigh_t = first_total[:, features : features + cols] + lacks
    lacks = lacks * SMALL
    lacks_xx = times(lacks, x_x)
    r_r = r_r - exact(lacks, r_x) - exact(r_x, lacks) + exact(lacks_xx, lacks)
    r_x = r_x - lacks_xx
    r_p = r_p - times(lacks, x_p)
    square = (cols, cols)
    eye = lax.broadcasted_iota(jnp.int32, square, 0) == lax.broadcasted_iota(jnp.int32, square, 1)
    lengths = jnp.where(eye, r_r, 0.0)

    def scaling(lengths):
        return lax.rsqrt(lengths * (1.0 / SMALL**2) + 1e-06) * (1.0 / SMALL)

    scale = scaling(jnp.sum(lengths, axis=1, keepdims=True))
    across = scaling(jnp.sum(lengths, axis=0, keepdims=True))
    u_image_x = (r_r * (1.0 / SMALL) + exact(r_x, rayleigh_t)) * scale
    u_x, u_p = r_x * scale, r_p * scale
    turned = exact(eye.astype(FLOAT), jnp.concatenate([rayleigh_t, u_image_x, image_x_p, u_x, x_p, u_p]))
    turned = [turned[:, i * cols : (i + 1) * cols] for i in range(6)]
    rows = [[x_x, turned[3], x_p], [u_x, r_r * scale * across, u_p], [turned[4], turned[5], p_p]]
    for i, row in enumerate(rows):
        search[i * cols : (i + 1) * cols] = jnp.concatenate(row, axis=1)
    return scale, across, eye.astype(FLOAT), turned[:3], u_image_x, image_x_p


def last_kernel(wide, gathered, first_total, found, known, images, gram, search):
    cols, features = found.shape[0], images.shape[1]
    scale, across, eye, turned, u_image_x, image_x_p = inner_products(wide, first_total, found, known, search)
    images[:cols] = first_total[:, :features]
    cross = []
    for d in range(gathered.shape[0]):
        rows = gathered[d, :, :features].astype(FLOAT)
        if 2 * d < cols:
            rows = rows * scale[2 * d : 2 * d + 2]
        images[cols + 2 * d : cols + 2 * d + 2] = rows
        pair = gathered[d, :, features:].astype(FLOAT)
        cross.append(pair[:1] + pair[1:])
    cross = jnp.concatenate(cross) * scale
    u_u, u_p = cross[:, :cols] * across, cross[:, cols:]
    p_p = first_total[:, features + cols :]
    rows = [
        [turned[0], turned[1], image_x_p],
        [u_image_x, u_u, u_p],
        [turned[2], exact(eye, u_p), p_p],
    ]
    for i, row in enumerate(rows):
        gram[i * cols : (i + 1) * cols] = jnp.concatenate(row, axis=1)


def local(hidden_states, current_block, directions):
    tokens, features = hidden_states.shape
    cols = current_block.shape[1]
    feat, tok = lax.axis_size("feat"), lax.axis_size("tok")
    factor = 0.5 / math.sqrt(tokens * tok - LAG)
    whole, wide = tokens // LANES * LANES, padded(tokens + LAG)

    behind = lax.ppermute(hidden_states[tokens - HALO :], "tok", [(i, i + 1) for i in range(tok - 1)])
    ahead = lax.ppermute(hidden_states[:HALO], "tok", [(i + 1, i) for i in range(tok - 1)])
    both = jnp.concatenate([current_block.T, directions.T])

    total = wide + 2 * cols
    flat = shape((2 * cols, total), HALF)
    part = kernel_call(start_kernel, flat, both, hidden_states)
    part = kernel_call(functools.partial(edge_kernel, whole), flat, both, hidden_states[whole:], behind, ahead, part)
    blocked = shape((feat, 2 * cols // feat, total), HALF)
    part = exchange(part.reshape(blocked.shape), "feat")
    part = kernel_call(functools.partial(known_kernel, wide), blocked, part)
    known = exchange(part, "feat").reshape(2 * cols, total)

    part = kernel_call(first_kernel, shape((cols, features + 2 * cols), FLOAT), known, hidden_states, behind, ahead)
    flat = shape((tok, cols * (features + 2 * cols) // tok), FLOAT)
    part = exchange(part.reshape(flat.shape), "tok")
    part = kernel_call(functools.partial(spread_kernel, factor), flat, part)
    part = exchange(part, "tok")
    first_total = part.reshape(cols, features + 2 * cols)

    total = wide + 12 * cols
    part = kernel_call(
        functools.partial(residual_kernel, feat), shape((cols, total), HALF), first_total, both, hidden_states, behind, ahead
    )
    blocked = shape((feat, cols // feat, total), HALF)
    part = exchange(part.reshape(blocked.shape), "feat")
    part = kernel_call(functools.partial(found_kernel, wide), blocked, part, known)
    found = exchange(part, "feat").reshape(cols, total)

    blocked = shape((tok, 2, features + 2 * cols), HALF)
    part = kernel_call(image_kernel, blocked, found, known, hidden_states, behind, ahead)
    part = exchange(part, "tok")
    part = kernel_call(functools.partial(total_kernel, factor, features), blocked, part)
    gathered = exchange(part, "tok")
    gram = shape((3 * cols, 3 * cols), FLOAT)
    images, gram_image, gram_search = kernel_call(
        functools.partial(last_kernel, wide),
        [shape((3 * cols, features), FLOAT), gram, gram],
        gathered,
        first_total,
        found,
        known,
    )
    return (images.T, gram_image, gram_search)


def solution(mesh):
    return jax.shard_map(
        local,
        mesh=mesh,
        in_specs=(P("tok", "feat"), P("feat", None), P("feat", None)),
        out_specs=(P("feat", None), P(), P()),
        check_vma=False,
    )
```

```python
import functools
import math

import jax
import jax.numpy as jnp
from jax import lax
from jax.experimental import pallas as pl
from jax.experimental.pallas import tpu as pltpu
from jax.sharding import Mesh
from jax.sharding import PartitionSpec as P

LAG = 256
HALO = LAG // 2
SMALL = 2.0**-20
LANES = 128
HIGHEST = lax.Precision.HIGHEST
HALF = jnp.bfloat16
FLOAT = jnp.float32


def padded(size):
    return -(-size // LANES) * LANES


def exchange(value, axis):
    return lax.all_to_all(value, axis, 0, 0, tiled=True)


def gathered_rows(part):
    part = exchange(part, "chip")
    part = part.reshape(-1, part.shape[2])
    return lax.all_gather(part, "core", axis=0, tiled=True)


def kernel_call(body, outputs, *operands):
    many = isinstance(outputs, list)
    spec = pl.BlockSpec(memory_space=pltpu.VMEM)
    return pl.pallas_call(
        body,
        out_shape=outputs,
        in_specs=[spec] * len(operands),
        out_specs=[spec] * len(outputs) if many else spec,
        compiler_params=pltpu.CompilerParams(vmem_limit_bytes=16 * 2**20),
    )(*operands)


def shape(dims, dtype):
    return jax.ShapeDtypeStruct(dims, dtype)


def rows_dot(a, b, precision=None):
    return lax.dot_general(a, b, (((1,), (1,)), ((), ())), preferred_element_type=FLOAT, precision=precision)


def exact(a, b):
    return rows_dot(a, b, HIGHEST)


def times(a, b):
    return jnp.dot(a, b, precision=HIGHEST, preferred_element_type=FLOAT)


def high_low(value):
    high = value.astype(HALF)
    return high, (value - high.astype(FLOAT)).astype(HALF)


def joined(value):
    value = value.astype(FLOAT)
    middle = value.shape[1] // 2
    return value[:, :middle] + value[:, middle:]


def project_own(vectors, hidden, out):
    whole = hidden.shape[0] // LANES * LANES
    out[:, HALO : HALO + whole] = rows_dot(vectors, hidden[:whole])


def project_edges(vectors, tail, behind, ahead, out):
    rows = vectors.shape[0]
    out[:, :HALO] = rows_dot(vectors, behind[...])
    value = rows_dot(vectors, jnp.concatenate([tail, ahead[...]]))
    spare = padded(value.shape[1]) - value.shape[1]
    if spare:
        value = jnp.concatenate([value, jnp.zeros((rows, spare), FLOAT)], axis=1)
    return value


def two_terms(value):
    high = value.astype(HALF).astype(FLOAT)
    left = lax.broadcasted_iota(jnp.int32, value.shape, 1) < value.shape[1] // 2
    return jnp.where(left, high, value - high).astype(HALF)


def start_kernel(both, hidden, out):
    rows = both.shape[0]
    cols, wide = rows // 2, out.shape[1] - rows
    project_own(both[...].astype(HALF), hidden, out)
    products = exact(both[...], both[...])
    turned = pltpu.roll(products, cols, 1)
    left = lax.broadcasted_iota(jnp.int32, (cols, rows), 1) < cols
    out[:cols, wide:] = jnp.where(left, products[:cols], turned[:cols])
    out[cols:, wide:] = jnp.where(left, turned[cols:], products[cols:])


def edge_kernel(whole, both, tail, behind, ahead, start, out):
    wide = out.shape[1] - both.shape[0]
    out[:, HALO : HALO + whole] = start[:, HALO : HALO + whole]
    out[:, wide:] = start[:, wide:]
    out[:, HALO + whole : wide] = project_edges(both[...].astype(HALF), tail[...], behind, ahead, out)


def chip_known_kernel(wide, received, out):
    rows = out.shape[1]
    for i in range(out.shape[0]):
        total = received[0, i * rows : (i + 1) * rows] + received[1, i * rows : (i + 1) * rows]
        out[i] = jnp.concatenate([total[:, :wide].astype(HALF), two_terms(total[:, wide:])], axis=1)


def chip_found_kernel(wide, received, out):
    rows = out.shape[1]
    for i in range(out.shape[0]):
        total = received[0, i * rows : (i + 1) * rows] + received[1, i * rows : (i + 1) * rows]
        out[i] = jnp.concatenate([total[:, :wide].astype(HALF), *high_low(total[:, wide:])], axis=1)


def known_kernel(wide, received, out):
    total = jnp.sum(received[...].astype(FLOAT), axis=0)
    products = total[:, wide:]
    products = two_terms(products + pltpu.roll(products, products.shape[1] // 2, 1))
    total = jnp.concatenate([total[:, :wide].astype(HALF), products], axis=1)
    out[...] = jnp.broadcast_to(total, out.shape)


def lag_image(projected, rows, hidden, behind, ahead):
    tokens = hidden.shape[0]
    whole = tokens // LANES * LANES
    cut = whole - HALO
    here, later = projected[:, :tokens], projected[:, LAG : LAG + tokens]
    edge = jnp.concatenate([hidden[whole:], ahead[...]])
    image = jnp.dot(later[:, HALO:], hidden[: tokens - HALO], preferred_element_type=FLOAT)
    image += jnp.dot(here[:, :cut], hidden[HALO:whole], preferred_element_type=FLOAT)
    image += jnp.dot(here[:, cut:], edge, preferred_element_type=FLOAT)
    image += jnp.dot(later[:, :HALO], behind[...], preferred_element_type=FLOAT)
    cross = rows_dot(rows[:, LAG : LAG + tokens], here) + rows_dot(rows[:, :tokens], later)
    return image, cross


def lag_cross(projected, tokens):
    here, later = projected[:, :tokens], projected[:, LAG : LAG + tokens]
    return rows_dot(later, here) + rows_dot(here, later)


def first_kernel(known, hidden, behind, ahead, out):
    tokens, features = hidden.shape
    cols = out.shape[0]
    image, cross = lag_image(known[:cols], known[:cols], hidden, behind, ahead)
    out[:, :features] = image
    out[:, features:] = jnp.concatenate([cross, lag_cross(known[cols:, : padded(tokens + LAG)], tokens)], axis=1)


def spread_kernel(factor, received, out):
    total = jnp.sum(received[...], axis=0, keepdims=True) * factor
    out[...] = jnp.broadcast_to(total, out.shape)


def residual_kernel(feat, total, both, hidden, behind, ahead, out):
    tokens, features = hidden.shape
    cols = total.shape[0]
    whole, at = tokens // LANES * LANES, padded(tokens + LAG)
    image = total[:, :features]
    residual = (image - times(total[:, features : features + cols], both[:cols])) * SMALL
    rounded = residual.astype(HALF)
    project_own(rounded, hidden, out)
    out[:, HALO + whole : at] = project_edges(rounded, hidden[whole:], behind, ahead, out)
    products = exact(jnp.concatenate([residual, image, both[:cols]]), jnp.concatenate([both[...], residual]))
    share = total[:, features : features + cols] * (1.0 / feat)
    lacks = products[cols : 2 * cols, : 2 * cols] - jnp.concatenate([share, jnp.zeros_like(share)], axis=1)
    own = jnp.concatenate([products[:cols, 2 * cols :], products[2 * cols :, cols : 2 * cols]], axis=1)
    for value in (products[:cols, : 2 * cols], lacks, own):
        out[:, at : at + 2 * cols] = value
        at += 2 * cols


def found_kernel(wide, received, known, out):
    rows = received.shape[1]
    cols = known.shape[0] // 2
    total = jnp.sum(received[...].astype(FLOAT), axis=0)
    products = joined(total[:, wide:])
    lacks = products[:, 2 * cols : 3 * cols] * SMALL
    lacks = jnp.concatenate([lacks, jnp.zeros_like(lacks)]).astype(HALF)
    shift = jnp.dot(lacks, known[:cols, :wide], preferred_element_type=FLOAT)[:rows]
    high, low = high_low(products)
    total = jnp.concatenate([(total[:, :wide] - shift).astype(HALF), high, low], axis=1)
    out[...] = jnp.broadcast_to(total, out.shape)


def image_kernel(found, known, hidden, behind, ahead, out):
    tokens, features = hidden.shape
    cols = found.shape[0]
    wide = padded(tokens + LAG)
    rows = found[:, :wide]
    image, cross = lag_image(jnp.concatenate([rows, known[cols:, :wide]]), rows, hidden, behind, ahead)
    image = image.astype(HALF)
    high = cross.astype(HALF).astype(FLOAT)
    low = cross - high
    for d in range(out.shape[0]):
        out[d, :, :features] = image[2 * d : 2 * d + 2]
        out[d, :, features:] = jnp.concatenate([high[d : d + 1], low[d : d + 1]]).astype(HALF)


def total_kernel(factor, features, received, out):
    total = jnp.sum(received[...].astype(FLOAT), axis=0) * factor
    cross = total[:1, features:] + total[1:, features:]
    high = cross.astype(HALF).astype(FLOAT)
    cross = jnp.concatenate([high, cross - high])
    total = jnp.concatenate([total[:, :features], cross], axis=1).astype(HALF)
    out[...] = jnp.broadcast_to(total, out.shape)


def inner_products(wide, first_total, found, known, search):
    cols = found.shape[0]
    products = joined(found[:, wide:])
    r_x, r_p, lacks, image_x_p, r_r, x_p = (products[:, i * cols : (i + 1) * cols] for i in range(6))
    products = joined(known[:, wide:])
    x_x, p_p = products[:cols], products[cols:]
    features = first_total.shape[1] - 2 * cols
    rayleigh_t = first_total[:, features : features + cols] + lacks
    lacks = lacks * SMALL
    lacks_xx = times(lacks, x_x)
    r_r = r_r - exact(lacks, r_x) - exact(r_x, lacks) + exact(lacks_xx, lacks)
    r_x = r_x - lacks_xx
    r_p = r_p - times(lacks, x_p)
    square = (cols, cols)
    eye = lax.broadcasted_iota(jnp.int32, square, 0) == lax.broadcasted_iota(jnp.int32, square, 1)
    lengths = jnp.where(eye, r_r, 0.0)

    def scaling(lengths):
        return lax.rsqrt(lengths * (1.0 / SMALL**2) + 1e-06) * (1.0 / SMALL)

    scale = scaling(jnp.sum(lengths, axis=1, keepdims=True))
    across = scaling(jnp.sum(lengths, axis=0, keepdims=True))
    u_image_x = (r_r * (1.0 / SMALL) + exact(r_x, rayleigh_t)) * scale
    u_x, u_p = r_x * scale, r_p * scale
    turned = exact(eye.astype(FLOAT), jnp.concatenate([rayleigh_t, u_image_x, image_x_p, u_x, x_p, u_p]))
    turned = [turned[:, i * cols : (i + 1) * cols] for i in range(6)]
    rows = [[x_x, turned[3], x_p], [u_x, r_r * scale * across, u_p], [turned[4], turned[5], p_p]]
    for i, row in enumerate(rows):
        search[i * cols : (i + 1) * cols] = jnp.concatenate(row, axis=1)
    return scale, across, eye.astype(FLOAT), turned[:3], u_image_x, image_x_p


def last_kernel(wide, gathered, first_total, found, known, images, gram, search):
    cols, features = found.shape[0], images.shape[1]
    scale, across, eye, turned, u_image_x, image_x_p = inner_products(wide, first_total, found, known, search)
    images[:cols] = first_total[:, :features]
    cross = []
    for d in range(gathered.shape[0]):
        rows = gathered[d, :, :features].astype(FLOAT)
        if 2 * d < cols:
            rows = rows * scale[2 * d : 2 * d + 2]
        images[cols + 2 * d : cols + 2 * d + 2] = rows
        pair = gathered[d, :, features:].astype(FLOAT)
        cross.append(pair[:1] + pair[1:])
    cross = jnp.concatenate(cross) * scale
    u_u, u_p = cross[:, :cols] * across, cross[:, cols:]
    p_p = first_total[:, features + cols :]
    rows = [
        [turned[0], turned[1], image_x_p],
        [u_image_x, u_u, u_p],
        [turned[2], exact(eye, u_p), p_p],
    ]
    for i, row in enumerate(rows):
        gram[i * cols : (i + 1) * cols] = jnp.concatenate(row, axis=1)


def local(hidden_states, current_block, directions):
    tokens, features = hidden_states.shape
    cols = current_block.shape[1]
    chips, cores, tok = lax.axis_size("chip"), lax.axis_size("core"), lax.axis_size("tok")
    factor = 0.5 / math.sqrt(tokens * tok - LAG)
    whole, wide = tokens // LANES * LANES, padded(tokens + LAG)

    behind = lax.ppermute(hidden_states[tokens - HALO :], "tok", [(i, i + 1) for i in range(tok - 1)])
    ahead = lax.ppermute(hidden_states[:HALO], "tok", [(i + 1, i) for i in range(tok - 1)])
    both = jnp.concatenate([current_block.T, directions.T])

    total = wide + 2 * cols
    whole = tokens // LANES * LANES
    flat = shape((cores * cols, total), FLOAT)
    part = kernel_call(start_kernel, flat, both, hidden_states)
    part = kernel_call(functools.partial(edge_kernel, whole), flat, both, hidden_states[whole:], behind, ahead, part)
    part = exchange(part.reshape(cores, cols, total), "core")
    blocked = shape((chips, cols // chips, total), HALF)
    part = kernel_call(functools.partial(chip_known_kernel, wide), blocked, part)
    part = exchange(part, "chip")
    part = kernel_call(functools.partial(known_kernel, wide), blocked, part)
    known = gathered_rows(part)

    part = kernel_call(first_kernel, shape((cols, features + 2 * cols), FLOAT), known, hidden_states, behind, ahead)
    flat = shape((tok, cols * (features + 2 * cols) // tok), FLOAT)
    part = exchange(part.reshape(flat.shape), "tok")
    part = kernel_call(functools.partial(spread_kernel, factor), flat, part)
    part = exchange(part, "tok")
    first_total = part.reshape(cols, features + 2 * cols)

    part = kernel_call(
        functools.partial(residual_kernel, chips * cores),
        shape((cols, wide + 6 * cols), FLOAT),
        first_total,
        both,
        hidden_states,
        behind,
        ahead,
    )
    part = exchange(part.reshape(cores, cols // cores, -1), "core")
    blocked = shape((chips, cols // (cores * chips), wide + 12 * cols), HALF)
    part = kernel_call(functools.partial(chip_found_kernel, wide), blocked, part)
    part = exchange(part, "chip")
    part = kernel_call(functools.partial(found_kernel, wide), blocked, part, known)
    found = gathered_rows(part)

    blocked = shape((tok, 2, features + 2 * cols), HALF)
    part = kernel_call(image_kernel, blocked, found, known, hidden_states, behind, ahead)
    part = exchange(part, "tok")
    part = kernel_call(functools.partial(total_kernel, factor, features), blocked, part)
    gathered = exchange(part, "tok")
    gram = shape((3 * cols, 3 * cols), FLOAT)
    images, gram_image, gram_search = kernel_call(
        functools.partial(last_kernel, wide),
        [shape((3 * cols, features), FLOAT), gram, gram],
        gathered,
        first_total,
        found,
        known,
    )
    return (images.T, gram_image, gram_search)


def solution(mesh):
    devices = mesh.devices.reshape(mesh.shape["tok"], -1, 2)
    feat = ("chip", "core")
    return jax.shard_map(
        local,
        mesh=Mesh(devices, ("tok",) + feat),
        in_specs=(P("tok", feat), P(feat, None), P(feat, None)),
        out_specs=(P(feat, None), P(), P()),
        check_vma=False,
    )
```

```python
import functools
import math

import jax
import jax.numpy as jnp
from jax import lax
from jax.experimental import pallas as pl
from jax.experimental.pallas import tpu as pltpu
from jax.sharding import Mesh
from jax.sharding import PartitionSpec as P

LAG = 256
HALO = LAG // 2
SMALL = 2.0**-20
LANES = 128
HIGHEST = lax.Precision.HIGHEST
HALF = jnp.bfloat16
FLOAT = jnp.float32


def padded(size):
    return -(-size // LANES) * LANES


def exchange(value, axis):
    return lax.all_to_all(value, axis, 0, 0, tiled=True)


def gathered_rows(part):
    part = exchange(part, "chip")
    part = part.reshape(-1, part.shape[2])
    return lax.all_gather(part, "core", axis=0, tiled=True)


def kernel_call(body, outputs, *operands):
    many = isinstance(outputs, list)
    spec = pl.BlockSpec(memory_space=pltpu.VMEM)
    return pl.pallas_call(
        body,
        out_shape=outputs,
        in_specs=[spec] * len(operands),
        out_specs=[spec] * len(outputs) if many else spec,
        compiler_params=pltpu.CompilerParams(vmem_limit_bytes=16 * 2**20),
    )(*operands)


def shape(dims, dtype):
    return jax.ShapeDtypeStruct(dims, dtype)


def rows_dot(a, b, precision=None):
    return lax.dot_general(a, b, (((1,), (1,)), ((), ())), preferred_element_type=FLOAT, precision=precision)


def exact(a, b):
    return rows_dot(a, b, HIGHEST)


def times(a, b):
    return jnp.dot(a, b, precision=HIGHEST, preferred_element_type=FLOAT)


def high_low(value):
    high = value.astype(HALF)
    return high, (value - high.astype(FLOAT)).astype(HALF)


def joined(value):
    value = value.astype(FLOAT)
    middle = value.shape[1] // 2
    return value[:, :middle] + value[:, middle:]


def folded(value, rows):
    return value if value.shape[0] == rows else value[:rows] + value[rows:]


def project_own(vectors, hidden, out):
    whole = hidden.shape[0] // LANES * LANES
    out[:, HALO : HALO + whole] = folded(rows_dot(vectors, hidden[:whole]), out.shape[0])


def project_edges(vectors, tail, behind, ahead, out):
    rows = out.shape[0]
    out[:, :HALO] = folded(rows_dot(vectors, behind[...]), rows)
    value = folded(rows_dot(vectors, jnp.concatenate([tail, ahead[...]])), rows)
    spare = padded(value.shape[1]) - value.shape[1]
    if spare:
        value = jnp.concatenate([value, jnp.zeros((rows, spare), FLOAT)], axis=1)
    return value


def two_terms(value):
    high = value.astype(HALF).astype(FLOAT)
    left = lax.broadcasted_iota(jnp.int32, value.shape, 1) < value.shape[1] // 2
    return jnp.where(left, high, value - high).astype(HALF)


def start_kernel(both, hidden, out):
    rows = both.shape[0]
    cols, wide = rows // 2, out.shape[1] - rows
    project_own(both[...].astype(HALF), hidden, out)
    products = exact(both[...], both[...])
    turned = pltpu.roll(products, cols, 1)
    left = lax.broadcasted_iota(jnp.int32, (cols, rows), 1) < cols
    out[:cols, wide:] = jnp.where(left, products[:cols], turned[:cols])
    out[cols:, wide:] = jnp.where(left, turned[cols:], products[cols:])


def edge_kernel(whole, both, tail, behind, ahead, start, out):
    wide = out.shape[1] - both.shape[0]
    out[:, HALO : HALO + whole] = start[:, HALO : HALO + whole]
    out[:, wide:] = start[:, wide:]
    out[:, HALO + whole : wide] = project_edges(both[...].astype(HALF), tail[...], behind, ahead, out)


def chip_known_kernel(wide, received, out):
    rows = out.shape[1]
    for i in range(out.shape[0]):
        total = received[0, i * rows : (i + 1) * rows] + received[1, i * rows : (i + 1) * rows]
        out[i] = jnp.concatenate([total[:, :wide].astype(HALF), two_terms(total[:, wide:])], axis=1)


def chip_found_kernel(wide, received, out):
    rows = out.shape[1]
    for i in range(out.shape[0]):
        total = received[0, i * rows : (i + 1) * rows] + received[1, i * rows : (i + 1) * rows]
        out[i] = jnp.concatenate([total[:, :wide].astype(HALF), *high_low(total[:, wide:])], axis=1)


def known_kernel(wide, received, out):
    total = jnp.sum(received[...].astype(FLOAT), axis=0)
    products = total[:, wide:]
    products = two_terms(products + pltpu.roll(products, products.shape[1] // 2, 1))
    total = jnp.concatenate([total[:, :wide].astype(HALF), products], axis=1)
    out[...] = jnp.broadcast_to(total, out.shape)


def lag_image(projected, rows, hidden, behind, ahead):
    tokens = hidden.shape[0]
    whole = tokens // LANES * LANES
    cut = whole - HALO
    here, later = projected[:, :tokens], projected[:, LAG : LAG + tokens]
    edge = jnp.concatenate([hidden[whole:], ahead[...]])
    image = jnp.dot(later[:, HALO:], hidden[: tokens - HALO], preferred_element_type=FLOAT)
    image += jnp.dot(here[:, :cut], hidden[HALO:whole], preferred_element_type=FLOAT)
    image += jnp.dot(here[:, cut:], edge, preferred_element_type=FLOAT)
    image += jnp.dot(later[:, :HALO], behind[...], preferred_element_type=FLOAT)
    cross = rows_dot(rows[:, LAG : LAG + tokens], here) + rows_dot(rows[:, :tokens], later)
    return image, cross


def lag_cross(projected, tokens):
    here, later = projected[:, :tokens], projected[:, LAG : LAG + tokens]
    return rows_dot(later, here) + rows_dot(here, later)


def first_kernel(known, hidden, behind, ahead, out):
    tokens, features = hidden.shape
    cols, middle = known.shape[0] // 2, features // 2
    image, cross = lag_image(known[:cols], known[:cols], hidden, behind, ahead)
    other = lag_cross(known[cols:, : padded(tokens + LAG)], tokens)
    upper = jnp.concatenate([image[:, :middle], cross], axis=1)
    lower = jnp.concatenate([image[:, middle:], other], axis=1)
    for d in range(out.shape[0]):
        out[d] = jnp.concatenate([upper[d : d + 1], lower[d : d + 1]]).astype(HALF)


def spread_kernel(factor, cols, received, out):
    total = jnp.sum(received[...].astype(FLOAT), axis=0) * factor
    middle = total.shape[1] - cols
    pieces = [total[i : i + 1, part] for part in (slice(0, middle), slice(middle, None)) for i in (0, 1)]
    out[...] = jnp.broadcast_to(jnp.concatenate(pieces, axis=1), out.shape)


def residual_kernel(feat, total, both, hidden, behind, ahead, out):
    tokens, features = hidden.shape
    cols = total.shape[0]
    whole, at = tokens // LANES * LANES, padded(tokens + LAG)
    image = total[:, :features]
    residual = (image - times(total[:, features : features + cols], both[:cols])) * SMALL
    terms = jnp.concatenate(high_low(residual))
    project_own(terms, hidden, out)
    out[:, HALO + whole : at] = project_edges(terms, hidden[whole:], behind, ahead, out)
    products = exact(jnp.concatenate([residual, image, both[:cols]]), jnp.concatenate([both[...], residual]))
    share = total[:, features : features + cols] * (1.0 / feat)
    lacks = products[cols : 2 * cols, : 2 * cols] - jnp.concatenate([share, jnp.zeros_like(share)], axis=1)
    own = jnp.concatenate([products[:cols, 2 * cols :], products[2 * cols :, cols : 2 * cols]], axis=1)
    for value in (products[:cols, : 2 * cols], lacks, own):
        out[:, at : at + 2 * cols] = value
        at += 2 * cols


def found_kernel(wide, received, known, out):
    rows = received.shape[1]
    cols = known.shape[0] // 2
    total = jnp.sum(received[...].astype(FLOAT), axis=0)
    products = joined(total[:, wide:])
    lacks = products[:, 2 * cols : 3 * cols] * SMALL
    lacks = jnp.concatenate([lacks, jnp.zeros_like(lacks)]).astype(HALF)
    shift = jnp.dot(lacks, known[:cols, :wide], preferred_element_type=FLOAT)[:rows]
    high, low = high_low(products)
    total = jnp.concatenate([(total[:, :wide] - shift).astype(HALF), high, low], axis=1)
    out[...] = jnp.broadcast_to(total, out.shape)


def image_kernel(found, known, hidden, behind, ahead, out):
    tokens, features = hidden.shape
    cols = found.shape[0]
    wide = padded(tokens + LAG)
    rows = found[:, :wide]
    image, cross = lag_image(jnp.concatenate([rows, known[cols:, :wide]]), rows, hidden, behind, ahead)
    image = image.astype(HALF)
    high = cross.astype(HALF).astype(FLOAT)
    low = cross - high
    for d in range(out.shape[0]):
        out[d, :, :features] = image[2 * d : 2 * d + 2]
        out[d, :, features:] = jnp.concatenate([high[d : d + 1], low[d : d + 1]]).astype(HALF)


def total_kernel(factor, features, received, out):
    total = jnp.sum(received[...].astype(FLOAT), axis=0) * factor
    cross = total[:1, features:] + total[1:, features:]
    high = cross.astype(HALF).astype(FLOAT)
    cross = jnp.concatenate([high, cross - high])
    total = jnp.concatenate([total[:, :features], cross], axis=1).astype(HALF)
    out[...] = jnp.broadcast_to(total, out.shape)


def inner_products(wide, first_total, found, known, search):
    cols = found.shape[0]
    products = joined(found[:, wide:])
    r_x, r_p, lacks, image_x_p, r_r, x_p = (products[:, i * cols : (i + 1) * cols] for i in range(6))
    products = joined(known[:, wide:])
    x_x, p_p = products[:cols], products[cols:]
    features = first_total.shape[1] - 2 * cols
    rayleigh_t = first_total[:, features : features + cols] + lacks
    lacks = lacks * SMALL
    lacks_xx = times(lacks, x_x)
    r_r = r_r - exact(lacks, r_x) - exact(r_x, lacks) + exact(lacks_xx, lacks)
    r_x = r_x - lacks_xx
    r_p = r_p - times(lacks, x_p)
    square = (cols, cols)
    eye = lax.broadcasted_iota(jnp.int32, square, 0) == lax.broadcasted_iota(jnp.int32, square, 1)
    lengths = jnp.where(eye, r_r, 0.0)

    def scaling(lengths):
        return lax.rsqrt(lengths * (1.0 / SMALL**2) + 1e-06) * (1.0 / SMALL)

    scale = scaling(jnp.sum(lengths, axis=1, keepdims=True))
    across = scaling(jnp.sum(lengths, axis=0, keepdims=True))
    u_image_x = (r_r * (1.0 / SMALL) + exact(r_x, rayleigh_t)) * scale
    u_x, u_p = r_x * scale, r_p * scale
    turned = exact(eye.astype(FLOAT), jnp.concatenate([rayleigh_t, u_image_x, image_x_p, u_x, x_p, u_p]))
    turned = [turned[:, i * cols : (i + 1) * cols] for i in range(6)]
    rows = [[x_x, turned[3], x_p], [u_x, r_r * scale * across, u_p], [turned[4], turned[5], p_p]]
    for i, row in enumerate(rows):
        search[i * cols : (i + 1) * cols] = jnp.concatenate(row, axis=1)
    return scale, across, eye.astype(FLOAT), turned[:3], u_image_x, image_x_p


def last_kernel(wide, gathered, first_total, found, known, images, gram, search):
    cols, features = found.shape[0], images.shape[1]
    scale, across, eye, turned, u_image_x, image_x_p = inner_products(wide, first_total, found, known, search)
    images[:cols] = first_total[:, :features]
    cross = []
    for d in range(gathered.shape[0]):
        rows = gathered[d, :, :features].astype(FLOAT)
        if 2 * d < cols:
            rows = rows * scale[2 * d : 2 * d + 2]
        images[cols + 2 * d : cols + 2 * d + 2] = rows
        pair = gathered[d, :, features:].astype(FLOAT)
        cross.append(pair[:1] + pair[1:])
    cross = jnp.concatenate(cross) * scale
    u_u, u_p = cross[:, :cols] * across, cross[:, cols:]
    p_p = first_total[:, features + cols :]
    rows = [
        [turned[0], turned[1], image_x_p],
        [u_image_x, u_u, u_p],
        [turned[2], exact(eye, u_p), p_p],
    ]
    for i, row in enumerate(rows):
        gram[i * cols : (i + 1) * cols] = jnp.concatenate(row, axis=1)


def local(hidden_states, current_block, directions):
    tokens, features = hidden_states.shape
    cols = current_block.shape[1]
    chips, cores, tok = lax.axis_size("chip"), lax.axis_size("core"), lax.axis_size("tok")
    factor = 0.5 / math.sqrt(tokens * tok - LAG)
    whole, wide = tokens // LANES * LANES, padded(tokens + LAG)

    behind = lax.ppermute(hidden_states[tokens - HALO :], "tok", [(i, i + 1) for i in range(tok - 1)])
    ahead = lax.ppermute(hidden_states[:HALO], "tok", [(i + 1, i) for i in range(tok - 1)])
    both = jnp.concatenate([current_block.T, directions.T])

    total = wide + 2 * cols
    whole = tokens // LANES * LANES
    flat = shape((cores * cols, total), FLOAT)
    part = kernel_call(start_kernel, flat, both, hidden_states)
    part = kernel_call(functools.partial(edge_kernel, whole), flat, both, hidden_states[whole:], behind, ahead, part)
    part = exchange(part.reshape(cores, cols, total), "core")
    blocked = shape((chips, cols // chips, total), HALF)
    part = kernel_call(functools.partial(chip_known_kernel, wide), blocked, part)
    part = exchange(part, "chip")
    part = kernel_call(functools.partial(known_kernel, wide), blocked, part)
    known = gathered_rows(part)

    blocked = shape((tok, 2, features // 2 + cols), HALF)
    part = kernel_call(first_kernel, blocked, known, hidden_states, behind, ahead)
    part = exchange(part, "tok")
    flat = shape((tok, features + 2 * cols), FLOAT)
    part = kernel_call(functools.partial(spread_kernel, factor, cols), flat, part)
    part = exchange(part, "tok")
    first_total = part.reshape(cols, features + 2 * cols)

    part = kernel_call(
        functools.partial(residual_kernel, chips * cores),
        shape((cols, wide + 6 * cols), FLOAT),
        first_total,
        both,
        hidden_states,
        behind,
        ahead,
    )
    part = exchange(part.reshape(cores, cols // cores, -1), "core")
    blocked = shape((chips, cols // (cores * chips), wide + 12 * cols), HALF)
    part = kernel_call(functools.partial(chip_found_kernel, wide), blocked, part)
    part = exchange(part, "chip")
    part = kernel_call(functools.partial(found_kernel, wide), blocked, part, known)
    found = gathered_rows(part)

    blocked = shape((tok, 2, features + 2 * cols), HALF)
    part = kernel_call(image_kernel, blocked, found, known, hidden_states, behind, ahead)
    part = exchange(part, "tok")
    part = kernel_call(functools.partial(total_kernel, factor, features), blocked, part)
    gathered = exchange(part, "tok")
    gram = shape((3 * cols, 3 * cols), FLOAT)
    images, gram_image, gram_search = kernel_call(
        functools.partial(last_kernel, wide),
        [shape((3 * cols, features), FLOAT), gram, gram],
        gathered,
        first_total,
        found,
        known,
    )
    return (images.T, gram_image, gram_search)


def solution(mesh):
    devices = mesh.devices.reshape(mesh.shape["tok"], -1, 2)
    feat = ("chip", "core")
    return jax.shard_map(
        local,
        mesh=Mesh(devices, ("tok",) + feat),
        in_specs=(P("tok", feat), P(feat, None), P(feat, None)),
        out_specs=(P(feat, None), P(), P()),
        check_vma=False,
    )
```

```python
import functools
import math

import jax
import jax.numpy as jnp
from jax import lax
from jax.experimental import pallas as pl
from jax.experimental.pallas import tpu as pltpu
from jax.sharding import Mesh
from jax.sharding import PartitionSpec as P

LAG = 256
HALO = LAG // 2
SMALL = 2.0**-20
LANES = 128
HIGHEST = lax.Precision.HIGHEST
HALF = jnp.bfloat16
FLOAT = jnp.float32


def padded(size):
    return -(-size // LANES) * LANES


def exchange(value, axis):
    return lax.all_to_all(value, axis, 0, 0, tiled=True)


def gathered_rows(part):
    part = exchange(part, "chip")
    part = part.reshape(-1, part.shape[2])
    return lax.all_gather(part, "core", axis=0, tiled=True)


def kernel_call(body, outputs, *operands):
    many = isinstance(outputs, list)
    spec = pl.BlockSpec(memory_space=pltpu.VMEM)
    return pl.pallas_call(
        body,
        out_shape=outputs,
        in_specs=[spec] * len(operands),
        out_specs=[spec] * len(outputs) if many else spec,
        compiler_params=pltpu.CompilerParams(vmem_limit_bytes=16 * 2**20),
    )(*operands)


def shape(dims, dtype):
    return jax.ShapeDtypeStruct(dims, dtype)


def rows_dot(a, b, precision=None):
    return lax.dot_general(a, b, (((1,), (1,)), ((), ())), preferred_element_type=FLOAT, precision=precision)


def exact(a, b):
    return rows_dot(a, b, HIGHEST)


def times(a, b):
    return jnp.dot(a, b, precision=HIGHEST, preferred_element_type=FLOAT)


def high_low(value):
    high = value.astype(HALF)
    return high, (value - high.astype(FLOAT)).astype(HALF)


def joined(value):
    value = value.astype(FLOAT)
    middle = value.shape[1] // 2
    return value[:, :middle] + value[:, middle:]


def folded(value, rows):
    return value if value.shape[0] == rows else value[:rows] + value[rows:]


def project_own(vectors, hidden, out):
    whole = hidden.shape[0] // LANES * LANES
    out[:, HALO : HALO + whole] = folded(rows_dot(vectors, hidden[:whole]), out.shape[0])


def project_edges(vectors, tail, behind, ahead, out):
    rows = out.shape[0]
    out[:, :HALO] = folded(rows_dot(vectors, behind[...]), rows)
    value = folded(rows_dot(vectors, jnp.concatenate([tail, ahead[...]])), rows)
    spare = padded(value.shape[1]) - value.shape[1]
    if spare:
        value = jnp.concatenate([value, jnp.zeros((rows, spare), FLOAT)], axis=1)
    return value


def two_terms(value):
    high = value.astype(HALF).astype(FLOAT)
    left = lax.broadcasted_iota(jnp.int32, value.shape, 1) < value.shape[1] // 2
    return jnp.where(left, high, value - high).astype(HALF)


def start_kernel(both, hidden, out):
    rows = both.shape[0]
    cols, wide = rows // 2, out.shape[1] - rows
    rounded = both[...].astype(HALF)
    project_own(rounded, hidden, out)
    tokens = hidden.shape[0]
    whole = tokens // LANES * LANES
    if tokens > whole:
        last = rows_dot(rounded, hidden[tokens - LANES :])
        out[:, HALO + whole : HALO + whole + LANES] = pltpu.roll(last, tokens - whole, 1)
    products = exact(both[...], both[...])
    turned = pltpu.roll(products, cols, 1)
    left = lax.broadcasted_iota(jnp.int32, (cols, rows), 1) < cols
    out[:cols, wide:] = jnp.where(left, products[:cols], turned[:cols])
    out[cols:, wide:] = jnp.where(left, turned[cols:], products[cols:])


def edge_kernel(tokens, both, behind, ahead, start, out):
    rows, whole = both.shape[0], tokens // LANES * LANES
    wide, rest = out.shape[1] - rows, tokens - whole
    out[:, HALO : HALO + whole] = start[:, HALO : HALO + whole]
    out[:, wide:] = start[:, wide:]
    rounded = both[...].astype(HALF)
    out[:, :HALO] = rows_dot(rounded, behind[...])
    pieces = [start[:, HALO + whole : HALO + whole + LANES][:, :rest]] if rest else []
    pieces.append(rows_dot(rounded, ahead[...]))
    spare = wide - HALO - tokens - HALO
    if spare:
        pieces.append(jnp.zeros((rows, spare), FLOAT))
    out[:, HALO + whole : wide] = jnp.concatenate(pieces, axis=1)


def chip_known_kernel(wide, received, out):
    rows = out.shape[1]
    for i in range(out.shape[0]):
        total = received[0, i * rows : (i + 1) * rows] + received[1, i * rows : (i + 1) * rows]
        out[i] = jnp.concatenate([total[:, :wide].astype(HALF), two_terms(total[:, wide:])], axis=1)


def chip_found_kernel(wide, received, out):
    rows = out.shape[1]
    for i in range(out.shape[0]):
        total = received[0, i * rows : (i + 1) * rows] + received[1, i * rows : (i + 1) * rows]
        out[i] = jnp.concatenate([total[:, :wide].astype(HALF), *high_low(total[:, wide:])], axis=1)


def known_kernel(wide, received, out):
    total = jnp.sum(received[...].astype(FLOAT), axis=0)
    products = total[:, wide:]
    products = two_terms(products + pltpu.roll(products, products.shape[1] // 2, 1))
    total = jnp.concatenate([total[:, :wide].astype(HALF), products], axis=1)
    out[...] = jnp.broadcast_to(total, out.shape)


def lag_image(projected, rows, hidden, behind, ahead):
    tokens = hidden.shape[0]
    whole = tokens // LANES * LANES
    cut = whole - HALO
    here, later = projected[:, :tokens], projected[:, LAG : LAG + tokens]
    edge = jnp.concatenate([hidden[whole:], ahead[...]])
    image = jnp.dot(later[:, HALO:], hidden[: tokens - HALO], preferred_element_type=FLOAT)
    image += jnp.dot(here[:, :cut], hidden[HALO:whole], preferred_element_type=FLOAT)
    image += jnp.dot(here[:, cut:], edge, preferred_element_type=FLOAT)
    image += jnp.dot(later[:, :HALO], behind[...], preferred_element_type=FLOAT)
    cross = rows_dot(rows[:, LAG : LAG + tokens], here) + rows_dot(rows[:, :tokens], later)
    return image, cross


def lag_cross(projected, tokens):
    here, later = projected[:, :tokens], projected[:, LAG : LAG + tokens]
    return rows_dot(later, here) + rows_dot(here, later)


def first_kernel(known, hidden, behind, ahead, out):
    tokens, features = hidden.shape
    cols, middle = known.shape[0] // 2, features // 2
    image, cross = lag_image(known[:cols], known[:cols], hidden, behind, ahead)
    other = lag_cross(known[cols:, : padded(tokens + LAG)], tokens)
    upper = jnp.concatenate([image[:, :middle], cross], axis=1)
    lower = jnp.concatenate([image[:, middle:], other], axis=1)
    for d in range(out.shape[0]):
        out[d] = jnp.concatenate([upper[d : d + 1], lower[d : d + 1]]).astype(HALF)


def spread_kernel(factor, cols, received, out):
    total = jnp.sum(received[...].astype(FLOAT), axis=0) * factor
    middle = total.shape[1] - cols
    pieces = [total[i : i + 1, part] for part in (slice(0, middle), slice(middle, None)) for i in (0, 1)]
    out[...] = jnp.broadcast_to(jnp.concatenate(pieces, axis=1), out.shape)


def residual_kernel(feat, total, both, hidden, behind, ahead, out):
    tokens, features = hidden.shape
    cols = total.shape[0]
    whole, at = tokens // LANES * LANES, padded(tokens + LAG)
    image = total[:, :features]
    residual = (image - times(total[:, features : features + cols], both[:cols])) * SMALL
    terms = jnp.concatenate(high_low(residual))
    project_own(terms, hidden, out)
    out[:, HALO + whole : at] = project_edges(terms, hidden[whole:], behind, ahead, out)
    products = exact(jnp.concatenate([residual, image, both[:cols]]), jnp.concatenate([both[...], residual]))
    share = total[:, features : features + cols] * (1.0 / feat)
    lacks = products[cols : 2 * cols, : 2 * cols] - jnp.concatenate([share, jnp.zeros_like(share)], axis=1)
    own = jnp.concatenate([products[:cols, 2 * cols :], products[2 * cols :, cols : 2 * cols]], axis=1)
    for value in (products[:cols, : 2 * cols], lacks, own):
        out[:, at : at + 2 * cols] = value
        at += 2 * cols


def found_kernel(wide, received, known, out):
    rows = received.shape[1]
    cols = known.shape[0] // 2
    total = jnp.sum(received[...].astype(FLOAT), axis=0)
    products = joined(total[:, wide:])
    lacks = products[:, 2 * cols : 3 * cols] * SMALL
    lacks = jnp.concatenate([lacks, jnp.zeros_like(lacks)]).astype(HALF)
    shift = jnp.dot(lacks, known[:cols, :wide], preferred_element_type=FLOAT)[:rows]
    high, low = high_low(products)
    total = jnp.concatenate([(total[:, :wide] - shift).astype(HALF), high, low], axis=1)
    out[...] = jnp.broadcast_to(total, out.shape)


def image_kernel(found, known, hidden, behind, ahead, out):
    tokens, features = hidden.shape
    cols = found.shape[0]
    wide = padded(tokens + LAG)
    rows = found[:, :wide]
    image, cross = lag_image(jnp.concatenate([rows, known[cols:, :wide]]), rows, hidden, behind, ahead)
    image = image.astype(HALF)
    high = cross.astype(HALF).astype(FLOAT)
    low = cross - high
    for d in range(out.shape[0]):
        out[d, :, :features] = image[2 * d : 2 * d + 2]
        out[d, :, features:] = jnp.concatenate([high[d : d + 1], low[d : d + 1]]).astype(HALF)


def total_kernel(factor, features, received, out):
    total = jnp.sum(received[...].astype(FLOAT), axis=0) * factor
    cross = total[:1, features:] + total[1:, features:]
    high = cross.astype(HALF).astype(FLOAT)
    cross = jnp.concatenate([high, cross - high])
    total = jnp.concatenate([total[:, :features], cross], axis=1).astype(HALF)
    out[...] = jnp.broadcast_to(total, out.shape)


def inner_products(wide, first_total, found, known, search):
    cols = found.shape[0]
    products = joined(found[:, wide:])
    r_x, r_p, lacks, image_x_p, r_r, x_p = (products[:, i * cols : (i + 1) * cols] for i in range(6))
    products = joined(known[:, wide:])
    x_x, p_p = products[:cols], products[cols:]
    features = first_total.shape[1] - 2 * cols
    rayleigh_t = first_total[:, features : features + cols] + lacks
    lacks = lacks * SMALL
    lacks_xx = times(lacks, x_x)
    r_r = r_r - exact(lacks, r_x) - exact(r_x, lacks) + exact(lacks_xx, lacks)
    r_x = r_x - lacks_xx
    r_p = r_p - times(lacks, x_p)
    square = (cols, cols)
    eye = lax.broadcasted_iota(jnp.int32, square, 0) == lax.broadcasted_iota(jnp.int32, square, 1)
    lengths = jnp.where(eye, r_r, 0.0)

    def scaling(lengths):
        return lax.rsqrt(lengths * (1.0 / SMALL**2) + 1e-06) * (1.0 / SMALL)

    scale = scaling(jnp.sum(lengths, axis=1, keepdims=True))
    across = scaling(jnp.sum(lengths, axis=0, keepdims=True))
    u_image_x = (r_r * (1.0 / SMALL) + exact(r_x, rayleigh_t)) * scale
    u_x, u_p = r_x * scale, r_p * scale
    turned = exact(eye.astype(FLOAT), jnp.concatenate([rayleigh_t, u_image_x, image_x_p, u_x, x_p, u_p]))
    turned = [turned[:, i * cols : (i + 1) * cols] for i in range(6)]
    rows = [[x_x, turned[3], x_p], [u_x, r_r * scale * across, u_p], [turned[4], turned[5], p_p]]
    for i, row in enumerate(rows):
        search[i * cols : (i + 1) * cols] = jnp.concatenate(row, axis=1)
    return scale, across, eye.astype(FLOAT), turned[:3], u_image_x, image_x_p


def last_kernel(wide, gathered, first_total, found, known, images, gram, search):
    cols, features = found.shape[0], images.shape[1]
    scale, across, eye, turned, u_image_x, image_x_p = inner_products(wide, first_total, found, known, search)
    images[:cols] = first_total[:, :features]
    cross = []
    for d in range(gathered.shape[0]):
        rows = gathered[d, :, :features].astype(FLOAT)
        if 2 * d < cols:
            rows = rows * scale[2 * d : 2 * d + 2]
        images[cols + 2 * d : cols + 2 * d + 2] = rows
        pair = gathered[d, :, features:].astype(FLOAT)
        cross.append(pair[:1] + pair[1:])
    cross = jnp.concatenate(cross) * scale
    u_u, u_p = cross[:, :cols] * across, cross[:, cols:]
    p_p = first_total[:, features + cols :]
    rows = [
        [turned[0], turned[1], image_x_p],
        [u_image_x, u_u, u_p],
        [turned[2], exact(eye, u_p), p_p],
    ]
    for i, row in enumerate(rows):
        gram[i * cols : (i + 1) * cols] = jnp.concatenate(row, axis=1)


def local(hidden_states, current_block, directions):
    tokens, features = hidden_states.shape
    cols = current_block.shape[1]
    chips, cores, tok = lax.axis_size("chip"), lax.axis_size("core"), lax.axis_size("tok")
    factor = 0.5 / math.sqrt(tokens * tok - LAG)
    wide = padded(tokens + LAG)

    behind = lax.ppermute(hidden_states[tokens - HALO :], "tok", [(i, i + 1) for i in range(tok - 1)])
    ahead = lax.ppermute(hidden_states[:HALO], "tok", [(i + 1, i) for i in range(tok - 1)])
    both = jnp.concatenate([current_block.T, directions.T])

    total = wide + 2 * cols
    flat = shape((cores * cols, total), FLOAT)
    part = kernel_call(start_kernel, flat, both, hidden_states)
    part = kernel_call(functools.partial(edge_kernel, tokens), flat, both, behind, ahead, part)
    part = exchange(part.reshape(cores, cols, total), "core")
    blocked = shape((chips, cols // chips, total), HALF)
    part = kernel_call(functools.partial(chip_known_kernel, wide), blocked, part)
    part = exchange(part, "chip")
    part = kernel_call(functools.partial(known_kernel, wide), blocked, part)
    known = gathered_rows(part)

    blocked = shape((tok, 2, features // 2 + cols), HALF)
    part = kernel_call(first_kernel, blocked, known, hidden_states, behind, ahead)
    part = exchange(part, "tok")
    flat = shape((tok, features + 2 * cols), FLOAT)
    part = kernel_call(functools.partial(spread_kernel, factor, cols), flat, part)
    part = exchange(part, "tok")
    first_total = part.reshape(cols, features + 2 * cols)

    part = kernel_call(
        functools.partial(residual_kernel, chips * cores),
        shape((cols, wide + 6 * cols), FLOAT),
        first_total,
        both,
        hidden_states,
        behind,
        ahead,
    )
    part = exchange(part.reshape(cores, cols // cores, -1), "core")
    blocked = shape((chips, cols // (cores * chips), wide + 12 * cols), HALF)
    part = kernel_call(functools.partial(chip_found_kernel, wide), blocked, part)
    part = exchange(part, "chip")
    part = kernel_call(functools.partial(found_kernel, wide), blocked, part, known)
    found = gathered_rows(part)

    blocked = shape((tok, 2, features + 2 * cols), HALF)
    part = kernel_call(image_kernel, blocked, found, known, hidden_states, behind, ahead)
    part = exchange(part, "tok")
    part = kernel_call(functools.partial(total_kernel, factor, features), blocked, part)
    gathered = exchange(part, "tok")
    gram = shape((3 * cols, 3 * cols), FLOAT)
    images, gram_image, gram_search = kernel_call(
        functools.partial(last_kernel, wide),
        [shape((3 * cols, features), FLOAT), gram, gram],
        gathered,
        first_total,
        found,
        known,
    )
    return (images.T, gram_image, gram_search)


def solution(mesh):
    devices = mesh.devices.reshape(mesh.shape["tok"], -1, 2)
    feat = ("chip", "core")
    return jax.shard_map(
        local,
        mesh=Mesh(devices, ("tok",) + feat),
        in_specs=(P("tok", feat), P(feat, None), P(feat, None)),
        out_specs=(P(feat, None), P(), P()),
        check_vma=False,
    )
```

```python
import functools
import math

import jax
import jax.numpy as jnp
from jax import lax
from jax.experimental import pallas as pl
from jax.experimental.pallas import tpu as pltpu
from jax.sharding import Mesh
from jax.sharding import PartitionSpec as P

LAG = 256
HALO = LAG // 2
SMALL = 2.0**-20
LANES = 128
HIGHEST = lax.Precision.HIGHEST
HALF = jnp.bfloat16
FLOAT = jnp.float32


def padded(size):
    return -(-size // LANES) * LANES


def exchange(value, axis):
    return lax.all_to_all(value, axis, 0, 0, tiled=True)


def gathered_rows(part):
    part = exchange(part, "chip")
    part = part.reshape(-1, part.shape[2])
    return lax.all_gather(part, "core", axis=0, tiled=True)


def kernel_call(body, outputs, *operands, reuse=None):
    many = isinstance(outputs, list)
    spec = pl.BlockSpec(memory_space=pltpu.VMEM)
    return pl.pallas_call(
        body,
        out_shape=outputs,
        in_specs=[spec] * len(operands),
        out_specs=[spec] * len(outputs) if many else spec,
        input_output_aliases={} if reuse is None else {reuse: 0},
        compiler_params=pltpu.CompilerParams(vmem_limit_bytes=16 * 2**20),
    )(*operands)


def shape(dims, dtype):
    return jax.ShapeDtypeStruct(dims, dtype)


def rows_dot(a, b, precision=None):
    return lax.dot_general(a, b, (((1,), (1,)), ((), ())), preferred_element_type=FLOAT, precision=precision)


def exact(a, b):
    return rows_dot(a, b, HIGHEST)


def times(a, b):
    return jnp.dot(a, b, precision=HIGHEST, preferred_element_type=FLOAT)


def high_low(value):
    high = value.astype(HALF)
    return high, (value - high.astype(FLOAT)).astype(HALF)


def joined(value):
    value = value.astype(FLOAT)
    middle = value.shape[1] // 2
    return value[:, :middle] + value[:, middle:]


def folded(value, rows):
    return value if value.shape[0] == rows else value[:rows] + value[rows:]


def project_own(vectors, hidden, out):
    whole = hidden.shape[0] // LANES * LANES
    out[:, HALO : HALO + whole] = folded(rows_dot(vectors, hidden[:whole]), out.shape[0])


def project_edges(vectors, tail, behind, ahead, out):
    rows = out.shape[0]
    out[:, :HALO] = folded(rows_dot(vectors, behind[...]), rows)
    value = folded(rows_dot(vectors, jnp.concatenate([tail, ahead[...]])), rows)
    spare = padded(value.shape[1]) - value.shape[1]
    if spare:
        value = jnp.concatenate([value, jnp.zeros((rows, spare), FLOAT)], axis=1)
    return value


def two_terms(value):
    high = value.astype(HALF).astype(FLOAT)
    left = lax.broadcasted_iota(jnp.int32, value.shape, 1) < value.shape[1] // 2
    return jnp.where(left, high, value - high).astype(HALF)


def start_kernel(both, hidden, out):
    rows = both.shape[0]
    cols, wide = rows // 2, out.shape[1] - rows
    rounded = both[...].astype(HALF)
    project_own(rounded, hidden, out)
    tokens = hidden.shape[0]
    whole = tokens // LANES * LANES
    if tokens > whole:
        last = rows_dot(rounded, hidden[tokens - LANES :])
        out[:, HALO + whole : HALO + whole + LANES] = pltpu.roll(last, tokens - whole, 1)
    products = exact(both[...], both[...])
    turned = pltpu.roll(products, cols, 1)
    left = lax.broadcasted_iota(jnp.int32, (cols, rows), 1) < cols
    out[:cols, wide:] = jnp.where(left, products[:cols], turned[:cols])
    out[cols:, wide:] = jnp.where(left, turned[cols:], products[cols:])


def edge_kernel(tokens, both, behind, ahead, start, out):
    rows, whole = both.shape[0], tokens // LANES * LANES
    wide, rest = out.shape[1] - rows, tokens - whole
    rounded = both[...].astype(HALF)
    out[:, :HALO] = rows_dot(rounded, behind[...])
    pieces = [start[:, HALO + whole : HALO + whole + LANES][:, :rest]] if rest else []
    pieces.append(rows_dot(rounded, ahead[...]))
    spare = wide - HALO - tokens - HALO
    if spare:
        pieces.append(jnp.zeros((rows, spare), FLOAT))
    out[:, HALO + whole : wide] = jnp.concatenate(pieces, axis=1)


def chip_known_kernel(wide, received, out):
    rows = out.shape[1]
    for i in range(out.shape[0]):
        total = received[0, i * rows : (i + 1) * rows] + received[1, i * rows : (i + 1) * rows]
        out[i] = jnp.concatenate([total[:, :wide].astype(HALF), two_terms(total[:, wide:])], axis=1)


def chip_found_kernel(wide, received, out):
    rows = out.shape[1]
    for i in range(out.shape[0]):
        total = received[0, i * rows : (i + 1) * rows] + received[1, i * rows : (i + 1) * rows]
        out[i] = jnp.concatenate([total[:, :wide].astype(HALF), *high_low(total[:, wide:])], axis=1)


def known_kernel(wide, received, out):
    total = jnp.sum(received[...].astype(FLOAT), axis=0)
    products = total[:, wide:]
    products = two_terms(products + pltpu.roll(products, products.shape[1] // 2, 1))
    total = jnp.concatenate([total[:, :wide].astype(HALF), products], axis=1)
    out[...] = jnp.broadcast_to(total, out.shape)


def lag_image(projected, rows, hidden, behind, ahead):
    tokens = hidden.shape[0]
    whole = tokens // LANES * LANES
    cut = whole - HALO
    here, later = projected[:, :tokens], projected[:, LAG : LAG + tokens]
    edge = jnp.concatenate([hidden[whole:], ahead[...]])
    image = jnp.dot(later[:, HALO:], hidden[: tokens - HALO], preferred_element_type=FLOAT)
    image += jnp.dot(here[:, :cut], hidden[HALO:whole], preferred_element_type=FLOAT)
    image += jnp.dot(here[:, cut:], edge, preferred_element_type=FLOAT)
    image += jnp.dot(later[:, :HALO], behind[...], preferred_element_type=FLOAT)
    cross = rows_dot(rows[:, LAG : LAG + tokens], here) + rows_dot(rows[:, :tokens], later)
    return image, cross


def lag_cross(projected, tokens):
    here, later = projected[:, :tokens], projected[:, LAG : LAG + tokens]
    return rows_dot(later, here) + rows_dot(here, later)


def first_kernel(known, hidden, behind, ahead, out):
    tokens, features = hidden.shape
    cols, middle = known.shape[0] // 2, features // 2
    image, cross = lag_image(known[:cols], known[:cols], hidden, behind, ahead)
    other = lag_cross(known[cols:, : padded(tokens + LAG)], tokens)
    upper = jnp.concatenate([image[:, :middle], cross], axis=1)
    lower = jnp.concatenate([image[:, middle:], other], axis=1)
    for d in range(out.shape[0]):
        out[d] = jnp.concatenate([upper[d : d + 1], lower[d : d + 1]]).astype(HALF)


def spread_kernel(factor, cols, received, out):
    total = jnp.sum(received[...].astype(FLOAT), axis=0) * factor
    middle = total.shape[1] - cols
    pieces = [total[i : i + 1, part] for part in (slice(0, middle), slice(middle, None)) for i in (0, 1)]
    out[...] = jnp.broadcast_to(jnp.concatenate(pieces, axis=1), out.shape)


def residual_kernel(feat, total, both, hidden, behind, ahead, out):
    tokens, features = hidden.shape
    cols = total.shape[0]
    whole, at = tokens // LANES * LANES, padded(tokens + LAG)
    image = total[:, :features]
    residual = (image - times(total[:, features : features + cols], both[:cols])) * SMALL
    terms = jnp.concatenate(high_low(residual))
    project_own(terms, hidden, out)
    out[:, HALO + whole : at] = project_edges(terms, hidden[whole:], behind, ahead, out)
    products = exact(jnp.concatenate([residual, image, both[:cols]]), jnp.concatenate([both[...], residual]))
    share = total[:, features : features + cols] * (1.0 / feat)
    lacks = products[cols : 2 * cols, : 2 * cols] - jnp.concatenate([share, jnp.zeros_like(share)], axis=1)
    own = jnp.concatenate([products[:cols, 2 * cols :], products[2 * cols :, cols : 2 * cols]], axis=1)
    for value in (products[:cols, : 2 * cols], lacks, own):
        out[:, at : at + 2 * cols] = value
        at += 2 * cols


def found_kernel(wide, received, known, out):
    rows = received.shape[1]
    cols = known.shape[0] // 2
    total = jnp.sum(received[...].astype(FLOAT), axis=0)
    products = joined(total[:, wide:])
    lacks = products[:, 2 * cols : 3 * cols] * SMALL
    lacks = jnp.concatenate([lacks, jnp.zeros_like(lacks)]).astype(HALF)
    shift = jnp.dot(lacks, known[:cols, :wide], preferred_element_type=FLOAT)[:rows]
    high, low = high_low(products)
    total = jnp.concatenate([(total[:, :wide] - shift).astype(HALF), high, low], axis=1)
    out[...] = jnp.broadcast_to(total, out.shape)


def image_kernel(found, known, hidden, behind, ahead, out):
    tokens, features = hidden.shape
    cols = found.shape[0]
    wide = padded(tokens + LAG)
    rows = found[:, :wide]
    image, cross = lag_image(jnp.concatenate([rows, known[cols:, :wide]]), rows, hidden, behind, ahead)
    image = image.astype(HALF)
    high = cross.astype(HALF).astype(FLOAT)
    low = cross - high
    for d in range(out.shape[0]):
        out[d, :, :features] = image[2 * d : 2 * d + 2]
        out[d, :, features:] = jnp.concatenate([high[d : d + 1], low[d : d + 1]]).astype(HALF)


def total_kernel(factor, features, received, out):
    total = jnp.sum(received[...].astype(FLOAT), axis=0) * factor
    cross = total[:1, features:] + total[1:, features:]
    high = cross.astype(HALF).astype(FLOAT)
    cross = jnp.concatenate([high, cross - high])
    total = jnp.concatenate([total[:, :features], cross], axis=1).astype(HALF)
    out[...] = jnp.broadcast_to(total, out.shape)


def inner_products(wide, first_total, found, known, search):
    cols = found.shape[0]
    products = joined(found[:, wide:])
    r_x, r_p, lacks, image_x_p, r_r, x_p = (products[:, i * cols : (i + 1) * cols] for i in range(6))
    products = joined(known[:, wide:])
    x_x, p_p = products[:cols], products[cols:]
    features = first_total.shape[1] - 2 * cols
    rayleigh_t = first_total[:, features : features + cols] + lacks
    lacks = lacks * SMALL
    lacks_xx = times(lacks, x_x)
    r_r = r_r - exact(lacks, r_x) - exact(r_x, lacks) + exact(lacks_xx, lacks)
    r_x = r_x - lacks_xx
    r_p = r_p - times(lacks, x_p)
    square = (cols, cols)
    eye = lax.broadcasted_iota(jnp.int32, square, 0) == lax.broadcasted_iota(jnp.int32, square, 1)
    lengths = jnp.where(eye, r_r, 0.0)

    def scaling(lengths):
        return lax.rsqrt(lengths * (1.0 / SMALL**2) + 1e-06) * (1.0 / SMALL)

    scale = scaling(jnp.sum(lengths, axis=1, keepdims=True))
    across = scaling(jnp.sum(lengths, axis=0, keepdims=True))
    u_image_x = (r_r * (1.0 / SMALL) + exact(r_x, rayleigh_t)) * scale
    u_x, u_p = r_x * scale, r_p * scale
    turned = exact(eye.astype(FLOAT), jnp.concatenate([rayleigh_t, u_image_x, image_x_p, u_x, x_p, u_p]))
    turned = [turned[:, i * cols : (i + 1) * cols] for i in range(6)]
    rows = [[x_x, turned[3], x_p], [u_x, r_r * scale * across, u_p], [turned[4], turned[5], p_p]]
    for i, row in enumerate(rows):
        search[i * cols : (i + 1) * cols] = jnp.concatenate(row, axis=1)
    return scale, across, eye.astype(FLOAT), turned[:3], u_image_x, image_x_p


def last_kernel(wide, gathered, first_total, found, known, images, gram, search):
    cols, features = found.shape[0], images.shape[1]
    scale, across, eye, turned, u_image_x, image_x_p = inner_products(wide, first_total, found, known, search)
    images[:cols] = first_total[:, :features]
    cross = []
    for d in range(gathered.shape[0]):
        rows = gathered[d, :, :features].astype(FLOAT)
        if 2 * d < cols:
            rows = rows * scale[2 * d : 2 * d + 2]
        images[cols + 2 * d : cols + 2 * d + 2] = rows
        pair = gathered[d, :, features:].astype(FLOAT)
        cross.append(pair[:1] + pair[1:])
    cross = jnp.concatenate(cross) * scale
    u_u, u_p = cross[:, :cols] * across, cross[:, cols:]
    p_p = first_total[:, features + cols :]
    rows = [
        [turned[0], turned[1], image_x_p],
        [u_image_x, u_u, u_p],
        [turned[2], exact(eye, u_p), p_p],
    ]
    for i, row in enumerate(rows):
        gram[i * cols : (i + 1) * cols] = jnp.concatenate(row, axis=1)


def local(hidden_states, current_block, directions):
    tokens, features = hidden_states.shape
    cols = current_block.shape[1]
    chips, cores, tok = lax.axis_size("chip"), lax.axis_size("core"), lax.axis_size("tok")
    factor = 0.5 / math.sqrt(tokens * tok - LAG)
    wide = padded(tokens + LAG)

    behind = lax.ppermute(hidden_states[tokens - HALO :], "tok", [(i, i + 1) for i in range(tok - 1)])
    ahead = lax.ppermute(hidden_states[:HALO], "tok", [(i + 1, i) for i in range(tok - 1)])
    both = jnp.concatenate([current_block.T, directions.T])

    total = wide + 2 * cols
    flat = shape((cores * cols, total), FLOAT)
    part = kernel_call(start_kernel, flat, both, hidden_states)
    part = kernel_call(functools.partial(edge_kernel, tokens), flat, both, behind, ahead, part, reuse=3)
    part = exchange(part.reshape(cores, cols, total), "core")
    blocked = shape((chips, cols // chips, total), HALF)
    part = kernel_call(functools.partial(chip_known_kernel, wide), blocked, part)
    part = exchange(part, "chip")
    part = kernel_call(functools.partial(known_kernel, wide), blocked, part)
    known = gathered_rows(part)

    blocked = shape((tok, 2, features // 2 + cols), HALF)
    part = kernel_call(first_kernel, blocked, known, hidden_states, behind, ahead)
    part = exchange(part, "tok")
    flat = shape((tok, features + 2 * cols), FLOAT)
    part = kernel_call(functools.partial(spread_kernel, factor, cols), flat, part)
    part = exchange(part, "tok")
    first_total = part.reshape(cols, features + 2 * cols)

    part = kernel_call(
        functools.partial(residual_kernel, chips * cores),
        shape((cols, wide + 6 * cols), FLOAT),
        first_total,
        both,
        hidden_states,
        behind,
        ahead,
    )
    part = exchange(part.reshape(cores, cols // cores, -1), "core")
    blocked = shape((chips, cols // (cores * chips), wide + 12 * cols), HALF)
    part = kernel_call(functools.partial(chip_found_kernel, wide), blocked, part)
    part = exchange(part, "chip")
    part = kernel_call(functools.partial(found_kernel, wide), blocked, part, known)
    found = gathered_rows(part)

    blocked = shape((tok, 2, features + 2 * cols), HALF)
    part = kernel_call(image_kernel, blocked, found, known, hidden_states, behind, ahead)
    part = exchange(part, "tok")
    part = kernel_call(functools.partial(total_kernel, factor, features), blocked, part)
    gathered = exchange(part, "tok")
    gram = shape((3 * cols, 3 * cols), FLOAT)
    images, gram_image, gram_search = kernel_call(
        functools.partial(last_kernel, wide),
        [shape((3 * cols, features), FLOAT), gram, gram],
        gathered,
        first_total,
        found,
        known,
    )
    return (images.T, gram_image, gram_search)


def solution(mesh):
    devices = mesh.devices.reshape(mesh.shape["tok"], -1, 2)
    feat = ("chip", "core")
    return jax.shard_map(
        local,
        mesh=Mesh(devices, ("tok",) + feat),
        in_specs=(P("tok", feat), P(feat, None), P(feat, None)),
        out_specs=(P(feat, None), P(), P()),
        check_vma=False,
    )
```
